128 devices in a mesh: seq: 16 (over x, z), tp: 8 (over y, core).
Axes of the slice: x: 4, y: 4, z: 4, core: 2. Of those that a mesh axis runs over, the one named last changes fastest.
Arguments:
- queries: bfloat16 [4096, 8192], P('seq', 'tp'), may hold values from -1000 to 1000
- states: bfloat16 [8192, 4096], P('seq', 'tp'), may hold values from -18 to 18
- state_doc: int32 [8192], replicated, may hold values from 0 to 15, as said below
- state_pos: int32 [8192], replicated, may hold values from 0 to 511, as said below
- lengths: int32 [16], replicated, may hold values from 64 to 512, as said below
- offsets: int32 [16], replicated, may hold values from 0 to 256
- key_weight: bfloat16 [4096, 8192], P(None, 'tp'), may hold values from -1 to 1
- value_weight: bfloat16 [4096, 8192], P(None, 'tp'), may hold values from -1 to 1
- context_grad: bfloat16 [4096, 8192], P('seq', 'tp'), may hold values from -6 to 6
Outputs:
- query_grad: bfloat16 [4096, 8192], P('seq', 'tp')
- key_weight_grad: bfloat16 [4096, 8192], P('seq', 'tp')
- value_weight_grad: bfloat16 [4096, 8192], P('seq', 'tp')
The draws below stay inside these ranges and needn't reach their ends.
Inputs may be any that keep to these rules, and one draw needn't show every extreme that they name: `state_doc`: each document has exactly 512 state rows. The 512 rows held by one index of seq name any one document at most 56 times, and in every draw some device's rows name some document exactly 56 times. `state_pos`: within one document the state rows carry each position from 0 to 511 exactly once. `lengths`: some document has length 512.
All inputs are finite; a program needn't handle non-finite values.
Results may differ from the reference program's by a relative error of at most 0.017.
Values may be sent and summed in bfloat16 or wider, within the bound.
A program may use at most 128 MiB of HBM per device.

```python
import jax
import jax.numpy as jnp
from jax import lax

D = 8192
HEADS = 64
HEAD_DIM = 128
DA = 4096
QDOC = 256
LDOC = 512
NDOC = 16
TOKENS = 4096
S_ROWS = 8192


def shuffle_one(subkey):
    return jax.random.permutation(subkey, LDOC)


def route_table(key):
    sigma = jax.random.permutation(jax.random.fold_in(key, 11), NDOC)
    base_count = 3 * LDOC // (4 * NDOC)
    lift_count = LDOC // 16
    nudge_count = base_count // 2
    sources = jnp.arange(NDOC)
    counts = jnp.full((NDOC, NDOC), base_count, jnp.int32)
    for step_shift, amount in ((0, lift_count), (1, lift_count), (2, lift_count), (3, lift_count), (4, nudge_count), (5, -nudge_count)):
        counts = counts.at[sources, sigma[(sources + step_shift) % NDOC]].add(amount)
    bounds = jnp.cumsum(counts, axis=1)
    slot_index = jnp.arange(LDOC)
    doc_of = jnp.sum((slot_index[None, :, None] >= bounds[:, None, :]).astype(jnp.int32), axis=2)
    shuffles = jax.vmap(shuffle_one)(jax.random.split(jax.random.fold_in(key, 12), NDOC))
    docs = jnp.take_along_axis(doc_of, shuffles, axis=1).reshape(-1)
    onehot = (docs[:, None] == jnp.arange(NDOC)[None, :]).astype(jnp.int32)
    ranks = jnp.sum((jnp.cumsum(onehot, axis=0) - onehot) * onehot, axis=1)
    position_perm = jax.vmap(shuffle_one)(jax.random.split(jax.random.fold_in(key, 13), NDOC))
    positions = position_perm[docs, ranks]
    return (docs.astype(jnp.int32), positions.astype(jnp.int32))


def state_table(key):
    docs, positions = route_table(key)
    raw_values = jnp.clip(jax.random.normal(jax.random.fold_in(key, 31), (S_ROWS, DA), jnp.float32), -6.0, 6.0)
    pairing = jax.random.permutation(jax.random.fold_in(key, 32), NDOC)
    column_block = jnp.arange(DA) // (DA // NDOC)
    boost = 1.0 + 2.0 * (column_block[None, :] == pairing[docs][:, None]).astype(jnp.float32)
    return raw_values * boost


def weight_table(key, salt):
    raw_values = jnp.clip(jax.random.normal(jax.random.fold_in(key, salt), (DA, D), jnp.float32), -6.0, 6.0)
    return (raw_values * DA ** (-0.5)).astype(jnp.bfloat16)


def draw_state_doc(key, part):
    return route_table(key)[0]


def draw_state_pos(key, part):
    return route_table(key)[1]


def draw_lengths(key, part):
    drawn = jax.random.randint(jax.random.fold_in(key, 21), (NDOC,), LDOC // 8, LDOC + 1)
    chosen = jax.random.randint(jax.random.fold_in(key, 22), (), 0, NDOC)
    return drawn.at[chosen].set(LDOC).astype(jnp.int32)


def draw_states(key, part):
    return state_table(key).astype(jnp.bfloat16)


def draw_key_weight(key, part):
    return weight_table(key, 41)


def draw_value_weight(key, part):
    return weight_table(key, 42)


def draw_context_grad(key, part):
    result = jnp.clip(jax.random.normal(jax.random.fold_in(key, 61), (TOKENS, D), jnp.float32), -6.0, 6.0)
    return result.astype(jnp.bfloat16)


def draw_queries(key, part):
    result = jnp.clip(jax.random.normal(jax.random.fold_in(key, 51), (TOKENS, D), jnp.float32), -6.0, 6.0)
    return jnp.clip(result, -1000.0, 1000.0).astype(jnp.bfloat16)


def place_ends(values, own_key, least, high):
    shape = values.shape
    place = [jax.random.randint(jax.random.fold_in(own_key, axis), (), 0, shape[axis]) for axis in range(len(shape))]
    values = values.at[tuple(place)].set(least)
    longest = shape.index(max(shape))
    place[longest] = (place[longest] + 1) % shape[longest]
    return values.at[tuple(place)].set(high)


def setup_inputs(seed: int = 0) -> dict:
    key_of = jax.random.split(jax.random.key(seed), 10)
    return {
        "queries": draw_queries(jax.random.fold_in(key_of[9], 71), 0),
        "states": draw_states(jax.random.fold_in(key_of[9], 71), 0),
        "state_doc": draw_state_doc(jax.random.fold_in(key_of[9], 71), 0),
        "state_pos": draw_state_pos(jax.random.fold_in(key_of[9], 71), 0),
        "lengths": draw_lengths(jax.random.fold_in(key_of[9], 71), 0),
        "offsets": place_ends(jax.random.randint(key_of[5], (NDOC,), 0, LDOC - QDOC + 1), jax.random.fold_in(key_of[5], 1), 0, LDOC - QDOC).astype(jnp.int32),
        "key_weight": draw_key_weight(jax.random.fold_in(key_of[9], 71), 0),
        "value_weight": draw_value_weight(jax.random.fold_in(key_of[9], 71), 0),
        "context_grad": draw_context_grad(jax.random.fold_in(key_of[9], 71), 0),
    }


def attend(query_rows, state_rows, positions, length, offset, key_weight, value_weight, grad_rows):
    key_rows = jnp.dot(state_rows, key_weight, preferred_element_type=jnp.float32).astype(jnp.bfloat16)
    value_rows = jnp.dot(state_rows, value_weight, preferred_element_type=jnp.float32).astype(jnp.bfloat16)
    query_count = query_rows.shape[0]
    state_count = state_rows.shape[0]
    query_heads = query_rows.reshape(query_count, HEADS, HEAD_DIM).astype(jnp.float32)
    key_heads = key_rows.reshape(state_count, HEADS, HEAD_DIM).astype(jnp.float32)
    value_heads = value_rows.reshape(state_count, HEADS, HEAD_DIM).astype(jnp.float32)
    grad_heads = grad_rows.reshape(query_count, HEADS, HEAD_DIM).astype(jnp.float32)
    score_scale = HEAD_DIM ** -0.5
    scores = jnp.einsum("qhd,khd->hqk", query_heads, key_heads) * score_scale
    query_index = jnp.arange(query_count)
    visible = (positions[None, :] <= offset + query_index[:, None]) & (positions[None, :] < length)
    scores = jnp.where(visible[None], scores, -jnp.inf)
    row_top = jnp.max(scores, axis=-1, keepdims=True)
    weights = jnp.exp(scores - row_top)
    probabilities = weights / jnp.sum(weights, axis=-1, keepdims=True)
    probs_low = probabilities.astype(jnp.bfloat16)
    probs_wide = probs_low.astype(jnp.float32)
    context = jnp.einsum("hqk,khd->qhd", probs_wide, value_heads)
    delta_rows = jnp.sum(grad_heads * context, axis=-1)
    prob_grad = jnp.einsum("qhd,khd->hqk", grad_heads, value_heads)
    score_grad = (probabilities * (prob_grad - delta_rows.T[:, :, None]) * score_scale).astype(jnp.bfloat16)
    score_wide = score_grad.astype(jnp.float32)
    query_grad = jnp.einsum("hqk,khd->qhd", score_wide, key_heads).astype(jnp.bfloat16)
    key_grad = jnp.einsum("hqk,qhd->khd", score_wide, query_heads).astype(jnp.bfloat16)
    value_grad = jnp.einsum("hqk,qhd->khd", probs_wide, grad_heads).astype(jnp.bfloat16)
    return (query_grad.reshape(query_count, D), key_grad.reshape(state_count, D),
            value_grad.reshape(state_count, D))


def reference(queries, states, state_doc, state_pos, lengths, offsets, key_weight, value_weight, context_grad):
    order = jnp.argsort(state_doc, stable=True)
    doc_states = jnp.take(states, order, axis=0).reshape(NDOC, LDOC, DA)
    doc_positions = jnp.take(state_pos, order, axis=0).reshape(NDOC, LDOC)
    doc_queries = queries.reshape(NDOC, QDOC, D)
    doc_grads = context_grad.reshape(NDOC, QDOC, D)

    def visit(totals, item):
        state_rows, positions, query_rows, grad_rows, length, offset = item
        query_grad, key_grad, value_grad = attend(query_rows, state_rows, positions, length, offset,
                                                  key_weight, value_weight, grad_rows)
        key_part = jnp.dot(state_rows.T, key_grad, preferred_element_type=jnp.float32).astype(jnp.bfloat16)
        value_part = jnp.dot(state_rows.T, value_grad, preferred_element_type=jnp.float32).astype(jnp.bfloat16)
        key_part, value_part = lax.optimization_barrier((key_part, value_part))
        return (totals[0] + key_part.astype(jnp.float32), totals[1] + value_part.astype(jnp.float32)), query_grad

    zeros = jnp.zeros((DA, D), jnp.float32)
    totals, query_grads = lax.scan(visit, (zeros, zeros),
                                   (doc_states, doc_positions, doc_queries, doc_grads, lengths, offsets))
    return (query_grads.reshape(TOKENS, D), totals[0].astype(jnp.bfloat16), totals[1].astype(jnp.bfloat16))
```

```python
import functools

import jax
import jax.numpy as jnp
from jax import lax
from jax.experimental import pallas as pl
from jax.experimental.pallas import tpu as pltpu
from jax.sharding import PartitionSpec as P

HEAD_DIM = 128
SLOTS = 64
F32 = jnp.float32
BF16 = jnp.bfloat16


def dot_nt(a, b):
    return lax.dot_general(a, b, (((1,), (1,)), ((), ())), preferred_element_type=F32)


def dot_tn(a, b):
    return lax.dot_general(a, b, (((0,), (0,)), ((), ())), preferred_element_type=F32)


def strict_upper(n):
    return (lax.broadcasted_iota(jnp.int32, (n, n), 0) < lax.broadcasted_iota(jnp.int32, (n, n), 1)).astype(F32).astype(BF16)


def pack_table(doc_ref, me, docs, rows):
    own = jnp.concatenate([doc_ref[pl.ds(4 * me + j, 1), :] for j in range(4)], axis=1)
    member = lax.broadcasted_iota(jnp.int32, (docs, rows), 0) == own
    member_f = member.astype(F32)
    ranks = jnp.dot(member_f.astype(BF16), strict_upper(rows), preferred_element_type=F32)
    rank = jnp.sum(ranks * member_f, axis=0, keepdims=True).astype(jnp.int32)
    target = own * SLOTS + rank
    hot = lax.broadcasted_iota(jnp.int32, (docs * SLOTS, rows), 0) == target
    return hot.astype(F32).astype(BF16)


def order_table(doc_ref, pos_ref, me, docs, rows):
    docs_all = jnp.concatenate([doc_ref[pl.ds(j, docs, stride=4), :] for j in range(4)], axis=1)
    pos_all = jnp.concatenate([pos_ref[pl.ds(j, docs, stride=4), :] for j in range(4)], axis=1)
    member = docs_all == me
    member_f = member.astype(F32)
    ranks = jnp.dot(member_f.astype(BF16), strict_upper(rows), preferred_element_type=F32).astype(jnp.int32)
    ranks = jnp.where(member, ranks, -1)
    high = (pos_all // 2).astype(F32)
    low = (pos_all % 2).astype(F32)
    parts = []
    for s in range(docs):
        hot = (lax.broadcasted_iota(jnp.int32, (SLOTS, rows), 0) == ranks[s:s + 1, :]).astype(F32).astype(BF16)
        three = jnp.concatenate([high[s:s + 1], low[s:s + 1], jnp.ones((1, rows), F32), jnp.zeros((5, rows), F32)], axis=0)
        parts.append(dot_nt(three.astype(BF16), hot))
    table = jnp.concatenate(parts, axis=1)
    slot_pos = (2.0 * table[0:1] + table[1:2] + table[2:3]).astype(jnp.int32) - 1
    hot = lax.broadcasted_iota(jnp.int32, (rows, docs * SLOTS), 0) == slot_pos
    return hot.astype(F32).astype(BF16)


def tables_kernel(docs, rows, doc_ref, pos_ref, pack_ref, order_ref):
    me = lax.axis_index("seq")
    pack_ref[...] = pack_table(doc_ref, me, docs, rows)
    order_ref[...] = order_table(doc_ref, pos_ref, me, docs, rows)


def attention_head(q, k, v, g, length, offset):
    scale = HEAD_DIM ** (-0.5)
    queries, rows = q.shape[0], k.shape[0]
    scores = dot_nt(q, k) * scale
    index = lax.broadcasted_iota(jnp.int32, (queries, rows), 0)
    pos = lax.broadcasted_iota(jnp.int32, (queries, rows), 1)
    visible = (pos <= index + offset) & (pos < length)
    scores = jnp.where(visible, scores, -jnp.inf)
    weights = jnp.exp(scores - jnp.max(scores, axis=1, keepdims=True))
    probs = weights * (1.0 / jnp.sum(weights, axis=1, keepdims=True))
    low = probs.astype(BF16)
    prob_grad = dot_nt(g, v)
    delta = jnp.sum(low.astype(F32) * prob_grad, axis=1, keepdims=True)
    score_grad = (probs * (prob_grad - delta) * scale).astype(BF16)
    q_grad = jnp.dot(score_grad, k, preferred_element_type=F32).astype(BF16)
    k_grad = dot_tn(q, score_grad).astype(BF16)
    v_grad = dot_tn(g, low).astype(BF16)
    return q_grad, k_grad, v_grad


def attention_kernel(len_ref, off_ref, q_ref, k_ref, v_ref, g_ref, qg_ref, kg_ref, vg_ref):
    me = lax.axis_index("seq")
    qg, kg, vg = attention_head(q_ref[...], k_ref[...], v_ref[...], g_ref[...], len_ref[me], off_ref[me])
    qg_ref[...] = qg
    kg_ref[...] = kg
    vg_ref[...] = vg


def attention(queries, keys, values, grads, lengths, offsets):
    count, width = queries.shape
    rows = keys.shape[0]
    col = lambda n: pl.BlockSpec((n, HEAD_DIM), lambda h, *_: (0, h))
    row = lambda n: pl.BlockSpec((HEAD_DIM, n), lambda h, *_: (h, 0))
    return pl.pallas_call(
        attention_kernel,
        grid_spec=pltpu.PrefetchScalarGridSpec(
            num_scalar_prefetch=2, grid=(width // HEAD_DIM,),
            in_specs=[col(count), col(rows), col(rows), col(count)],
            out_specs=[col(count), row(rows), row(rows)]),
        out_shape=[jax.ShapeDtypeStruct((count, width), BF16), jax.ShapeDtypeStruct((width, rows), BF16),
                   jax.ShapeDtypeStruct((width, rows), BF16)],
        cost_estimate=pl.CostEstimate(flops=12 * count * rows * width, bytes_accessed=8 * rows * width, transcendentals=0),
        name="attention",
    )(lengths, offsets, queries, keys, values, grads)


def shards(queries, states, state_doc, state_pos, lengths, offsets, key_weight, value_weight, context_grad):
    docs = lax.axis_size("seq")
    rows = states.shape[0]
    pack, order = pl.pallas_call(
        functools.partial(tables_kernel, docs, rows),
        out_shape=[jax.ShapeDtypeStruct((docs * SLOTS, rows), BF16), jax.ShapeDtypeStruct((rows, docs * SLOTS), BF16)],
        in_specs=[pl.BlockSpec(memory_space=pltpu.VMEM)] * 2,
        out_specs=[pl.BlockSpec(memory_space=pltpu.VMEM)] * 2,
        name="tables",
    )(state_doc.reshape(-1, 128), state_pos.reshape(-1, 128))
    packed = jnp.dot(pack, states, preferred_element_type=F32).astype(BF16)
    arrived = lax.all_to_all(packed, "seq", split_axis=0, concat_axis=0, tiled=True)
    own = jnp.dot(order, arrived, preferred_element_type=F32).astype(BF16)
    doc_states = lax.all_gather(own, "tp", axis=1, tiled=True)
    key_rows = jnp.dot(doc_states, key_weight, preferred_element_type=F32).astype(BF16)
    value_rows = jnp.dot(doc_states, value_weight, preferred_element_type=F32).astype(BF16)
    query_grad, key_grad, value_grad = attention(queries, key_rows, value_rows, context_grad, lengths, offsets)
    both = jnp.concatenate([key_grad, value_grad], axis=0)
    parts = lax.dot_general(doc_states, both, (((0,), (1,)), ((), ())), preferred_element_type=F32).astype(BF16)
    summed = lax.psum_scatter(parts, "seq", scatter_dimension=0, tiled=True)
    width = key_weight.shape[1]
    return query_grad, summed[:, :width], summed[:, width:]


def solution(mesh):
    in_specs = (P("seq", "tp"), P("seq", "tp"), P(), P(), P(), P(), P(None, "tp"), P(None, "tp"), P("seq", "tp"))
    out_specs = (P("seq", "tp"), P("seq", "tp"), P("seq", "tp"))
    return jax.shard_map(shards, mesh=mesh, in_specs=in_specs, out_specs=out_specs, check_vma=False)
```

```python
import functools

import jax
import jax.numpy as jnp
from jax import lax
from jax.experimental import pallas as pl
from jax.experimental.pallas import tpu as pltpu
from jax.sharding import PartitionSpec as P

HEAD_DIM = 128
SLOTS = 64
F32 = jnp.float32
BF16 = jnp.bfloat16


def dot_nt(a, b):
    return lax.dot_general(a, b, (((1,), (1,)), ((), ())), preferred_element_type=F32)


def dot_tn(a, b):
    return lax.dot_general(a, b, (((0,), (0,)), ((), ())), preferred_element_type=F32)


def strict_upper(n):
    return (lax.broadcasted_iota(jnp.int32, (n, n), 0) < lax.broadcasted_iota(jnp.int32, (n, n), 1)).astype(F32).astype(BF16)


def pack_table(doc_ref, me, docs, rows):
    own = jnp.concatenate([doc_ref[pl.ds(4 * me + j, 1), :] for j in range(4)], axis=1)
    member = lax.broadcasted_iota(jnp.int32, (docs, rows), 0) == own
    member_f = member.astype(F32)
    ranks = jnp.dot(member_f.astype(BF16), strict_upper(rows), preferred_element_type=F32)
    rank = jnp.sum(ranks * member_f, axis=0, keepdims=True).astype(jnp.int32)
    target = own * SLOTS + rank
    hot = lax.broadcasted_iota(jnp.int32, (docs * SLOTS, rows), 0) == target
    return hot.astype(F32).astype(BF16)


def order_table(doc_ref, pos_ref, me, docs, rows):
    docs_all = jnp.concatenate([doc_ref[pl.ds(j, docs, stride=4), :] for j in range(4)], axis=1)
    pos_all = jnp.concatenate([pos_ref[pl.ds(j, docs, stride=4), :] for j in range(4)], axis=1)
    member = docs_all == me
    member_f = member.astype(F32)
    ranks = jnp.dot(member_f.astype(BF16), strict_upper(rows), preferred_element_type=F32).astype(jnp.int32)
    ranks = jnp.where(member, ranks, -1)
    high = (pos_all // 2).astype(F32)
    low = (pos_all % 2).astype(F32)
    parts = []
    for s in range(docs):
        hot = (lax.broadcasted_iota(jnp.int32, (SLOTS, rows), 0) == ranks[s:s + 1, :]).astype(F32).astype(BF16)
        three = jnp.concatenate([high[s:s + 1], low[s:s + 1], jnp.ones((1, rows), F32), jnp.zeros((5, rows), F32)], axis=0)
        parts.append(dot_nt(three.astype(BF16), hot))
    table = jnp.concatenate(parts, axis=1)
    slot_pos = (2.0 * table[0:1] + table[1:2] + table[2:3]).astype(jnp.int32) - 1
    hot = lax.broadcasted_iota(jnp.int32, (rows, docs * SLOTS), 0) == slot_pos
    return hot.astype(F32).astype(BF16)


def attention_head(q, k, v, g, length, offset):
    scale = HEAD_DIM ** (-0.5)
    queries, rows = q.shape[0], k.shape[0]
    scores = dot_nt(q, k) * scale
    index = lax.broadcasted_iota(jnp.int32, (queries, rows), 0)
    pos = lax.broadcasted_iota(jnp.int32, (queries, rows), 1)
    visible = (pos <= index + offset) & (pos < length)
    scores = jnp.where(visible, scores, -jnp.inf)
    weights = jnp.exp(scores - jnp.max(scores, axis=1, keepdims=True))
    probs = weights * (1.0 / jnp.sum(weights, axis=1, keepdims=True))
    low = probs.astype(BF16)
    prob_grad = dot_nt(g, v)
    delta = jnp.sum(low.astype(F32) * prob_grad, axis=1, keepdims=True)
    score_grad = (probs * (prob_grad - delta) * scale).astype(BF16)
    q_grad = jnp.dot(score_grad, k, preferred_element_type=F32).astype(BF16)
    k_grad = dot_tn(q, score_grad).astype(BF16)
    v_grad = dot_tn(g, low).astype(BF16)
    return q_grad, k_grad, v_grad


MESH = pl.DeviceIdType.MESH
WSLOTS = 5


class Send:
    def __init__(self, src, dst, sems, index, seq, tp):
        send, recv = sems
        self.copy = pltpu.make_async_remote_copy(
            src_ref=src, dst_ref=dst, send_sem=send.at[index], recv_sem=recv.at[index],
            device_id={"seq": seq, "tp": tp}, device_id_type=MESH)

    def start(self):
        self.copy.start()
        return self

    def arrived(self):
        self.copy.wait_recv()

    def left(self):
        self.copy.wait_send()


def kernel(docs, doc_ref, pos_ref, len_ref, off_ref, q_hbm, s_hbm, wk_hbm, wv_hbm, g_hbm,
           qg_out, kw_out, vw_out,
           states, queries, grads, weights, packed, arrived, own, acc, kv, gown, gfar, sfar,
           far_out, far_in, near_out, near_in,
           load_sem, w_sem, a_send, a_recv, b_send, b_recv, c_send, c_recv, d_send, d_recv,
           g_send, g_recv, f_send, f_recv, r_send, r_recv, n_send, n_recv):
    rows = states.shape[0]
    me, tp = lax.axis_index("seq"), lax.axis_index("tp")
    x, z = me // 4, me % 4
    y, core = tp // 2, tp % 2

    def ring(v, k):
        return (v + k % 4) % 4

    def at_x(k):
        return ring(x, k) * 4 + z

    def at_z(k):
        return x * 4 + ring(z, k)

    def at_y(k, c=None):
        return ring(y, k) * 2 + (core if c is None else c)

    other = 1 - core
    partner = y * 2 + other
    line = (at_x, at_z)
    cross = (at_z, at_x)
    spot = (x, z)
    cross_spot = (z, x)

    loads = [pltpu.make_async_copy(s, d, load_sem.at[i])
             for i, (s, d) in enumerate(((s_hbm, states), (q_hbm, queries), (g_hbm, grads)))]
    for load in loads:
        load.start()
    slices = [at_y(0), partner, at_y(-1), at_y(1), at_y(-1, other), at_y(1, other), at_y(2), at_y(2, other)]

    def weight_loads(i):
        slot = i % WSLOTS
        return [pltpu.make_async_copy(w.at[slices[i]], weights.at[slot, p], w_sem.at[slot, p])
                for p, w in enumerate((wk_hbm, wv_hbm))]

    for i in range(WSLOTS):
        for load in weight_loads(i):
            load.start()

    barrier = pltpu.get_barrier_semaphore()
    for k in range(1, docs):
        pl.semaphore_signal(barrier, inc=1, device_id={"seq": (me + k) % docs, "tp": tp}, device_id_type=MESH)
    for t in (at_y(1), at_y(-1), partner):
        pl.semaphore_signal(barrier, inc=1, device_id={"seq": me, "tp": t}, device_id_type=MESH)

    table = pack_table(doc_ref, me, docs, rows)
    loads[0].wait()
    for h in range(2):
        block = jnp.dot(table, states[:, 256 * h:256 * h + 256], preferred_element_type=F32).astype(BF16)
        packed[h] = block.reshape(docs, SLOTS, 256)
    pl.semaphore_wait(barrier, docs - 1 + 3)
    routes = [[], []]
    for h in range(2):
        for k in range(1, docs):
            to = (me + k) % docs
            routes[h].append(Send(packed.at[h, to], arrived.at[h, me], (a_send, a_recv), (h, k), to, tp).start())
        arrived[h, me] = packed[h, me]
    table = order_table(doc_ref, pos_ref, me, docs, rows)

    gather = [{}, {}]
    for h in range(2):
        for route in routes[h]:
            route.arrived()
        own[2 * tp + h] = jnp.dot(table, arrived[h].reshape(docs * SLOTS, 256), preferred_element_type=F32).astype(BF16)
        piece = own.at[2 * tp + h]
        for i, t in enumerate((at_y(1), at_y(-1), partner)):
            gather[h][i] = Send(piece, piece, (b_send, b_recv), (h, i), me, t).start()

    def pass_on(h, i, origin, to):
        piece = own.at[2 * origin + h]
        gather[h][i] = Send(piece, piece, (b_send, b_recv), (h, i), me, to).start()

    def project(i):
        for load in weight_loads(i):
            load.wait()
        slot, part = i % WSLOTS, slices[i]
        last = i == len(slices) - 1

        def step(n, carry):
            p, j = n // 4, n % 4
            cols = pl.ds(pl.multiple_of(j * 256, 256), 256)
            left = jnp.concatenate([own[2 * part], own[2 * part + 1]], axis=1)
            value = jnp.dot(left, weights[slot, p, :, cols], preferred_element_type=F32)
            if i > 0:
                value = acc[p, j, :rows, :] + value
            if last:
                kv[p, :, cols] = value.astype(BF16)
            else:
                acc[p, j, :rows, :] = value
            return carry

        lax.fori_loop(0, 8, step, 0)
        if i + WSLOTS < len(slices):
            for load in weight_loads(i + WSLOTS):
                load.start()

    project(0)
    for h in range(2):
        gather[h][2].arrived()
    project(1)
    gather[0][0].arrived()
    pass_on(0, 3, at_y(-1), at_y(1))
    pass_on(0, 4, at_y(-1), partner)
    gather[0][1].arrived()
    pass_on(0, 5, at_y(1), partner)
    gather[1][1].arrived()
    pass_on(1, 3, at_y(1), at_y(-1))
    pass_on(1, 5, at_y(1), partner)
    gather[1][0].arrived()
    pass_on(1, 4, at_y(-1), partner)
    project(2)
    project(3)
    for h in range(2):
        gather[h][4].arrived()
        gather[h][5].arrived()
    project(4)
    for h in range(2):
        gather[h][3].arrived()
        pass_on(h, 6, at_y(2), partner)
    project(5)
    for h in range(2):
        gather[h][6].arrived()

    mine = pl.ds(pl.multiple_of(tp * 64, 64), 64)

    view = own.reshape(4, 4, rows, 256)

    def wanted(p, k, span):
        return view.at[ring(x, k), :, span, :] if p == 0 else view.at[:, ring(z, k), span, :]

    spread = {}
    for p in range(2):
        for slot, k in ((0, 1), (2, -1), (1, 2)):
            spread[p, slot] = Send(wanted(p, k, mine), sfar.at[p, slot, :, mine, :], (c_send, c_recv), (p, slot),
                                   line[p](k), tp).start()
    project(6)
    project(7)
    for load in loads[1:]:
        load.wait()

    second = {}

    def part_of(p, origin, js=None):
        span = pl.ds(pl.multiple_of(origin * 64, 64), 64)
        return sfar.at[p, :, :, span, :] if js is None else sfar.at[p, :, js, span, :]

    def hand(p, i, origin, to, js=None):
        piece = part_of(p, origin, js)
        second[p, i] = Send(piece, piece, (d_send, d_recv), (p, i), me, to).start()

    def second_own(p):
        for slot in range(3):
            spread[p, slot].arrived()
        for i, t in enumerate((at_y(1), at_y(-1), partner)):
            hand(p, i, tp, t)

    def second_near(p):
        second[p, 0].arrived()
        hand(p, 3, at_y(-1), at_y(1), pl.ds(0, 2))
        hand(p, 4, at_y(-1), partner)
        second[p, 1].arrived()
        hand(p, 7, at_y(1), at_y(-1), pl.ds(2, 2))
        hand(p, 5, at_y(1), partner)

    def second_far(p):
        second[p, 3].arrived()
        second[p, 7].arrived()
        hand(p, 6, at_y(2), partner)

    def second_all(p):
        for i in (2, 4, 5, 6):
            second[p, i].arrived()

    length, offset = len_ref[me], off_ref[me]
    shared = {}
    for chunk in range(4):
        def head(i, carry):
            at = pl.multiple_of((2 * chunk + i) * HEAD_DIM, HEAD_DIM)
            cols = pl.ds(at, HEAD_DIM)
            qg, kg, vg = attention_head(queries[:, cols], kv[0, :, cols], kv[1, :, cols], grads[:, cols], length, offset)
            qg_out[:, cols] = qg
            gown[0, cols, :] = kg
            gown[1, cols, :] = vg
            return carry

        lax.fori_loop(0, 2, head, 0)
        span = pl.ds(256 * chunk, 256)
        for p in range(2):
            for side, (k, slot) in enumerate(((1, 0), (-1, 2))):
                shared[p, chunk, side] = Send(gown.at[p, span, :], gfar.at[p, slot, span, :], (g_send, g_recv),
                                              (p, chunk, side), line[p](k), tp).start()
        if chunk == 2:
            second_own(0)

    passed = {}

    def forward(p, chunk):
        side = 0 if chunk < 2 else 1
        k, slot = ((1, 0), (-1, 2))[side]
        span = pl.ds(256 * chunk, 256)
        shared[p, chunk, side].arrived()
        passed[p, chunk] = Send(gfar.at[p, slot, span, :], gfar.at[p, 1, span, :], (f_send, f_recv), (p, chunk),
                                line[p](k), tp).start()

    def multiply(p, grad, state, first=False):
        def step(n, carry):
            half, j = n // 4, n % 4
            span = pl.ds(pl.multiple_of(half * 512, 512), 512)
            value = jnp.dot(grad[span, :], state(j), preferred_element_type=F32)
            acc[p, j, span, :] = value if first else acc[p, j, span, :] + value
            return carry

        lax.fori_loop(0, 8, step, 0)

    def mine_for(p):
        return (lambda j: own[4 * x + j]) if p == 0 else (lambda j: own[4 * j + z])

    def theirs(p, slot):
        return lambda j: sfar[p, slot, j]

    def near_docs(p):
        for side, slot in ((0, 0), (1, 2)):
            for chunk in range(4):
                if (chunk < 2) != (side == 0):
                    shared[p, chunk, side].arrived()
            multiply(p, gfar.at[p, slot], theirs(p, slot))

    multiply(0, gown.at[0], mine_for(0), True)
    second_near(0)
    second_own(1)
    multiply(1, gown.at[1], mine_for(1), True)
    for p in range(2):
        forward(p, 0)
        forward(p, 1)
    second_far(0)
    second_all(0)
    for p in range(2):
        forward(p, 2)
        forward(p, 3)
    near_docs(0)
    second_near(1)
    second_far(1)
    second_all(1)
    near_docs(1)

    top, bottom = pl.ds(0, 512), pl.ds(512, 512)

    def total(p, k, span):
        j = ring(cross_spot[p], k)
        return acc[p, j, span, :] + jnp.dot(gfar[p, 1, span, :], sfar[p, 1, j], preferred_element_type=F32)

    sums = {}

    def give(p, i, src, dst, k, sems):
        sums[p, i] = Send(src, dst, sems, (p, i), cross[p](k), tp).start()

    for p in range(2):
        for chunk in range(4):
            passed[p, chunk].arrived()
        far_out[p, 0] = total(p, 2, top).astype(BF16)
        far_out[p, 1] = total(p, 2, bottom).astype(BF16)
        give(p, 0, far_out.at[p, 0], far_in.at[p, 0], 1, (r_send, r_recv))
        give(p, 1, far_out.at[p, 1], far_in.at[p, 1], -1, (r_send, r_recv))
    for p in range(2):
        near_out[p, 0, 1] = total(p, 1, bottom).astype(BF16)
        near_out[p, 1, 0] = total(p, -1, top).astype(BF16)
        sums[p, 3] = Send(near_out.at[p, 0, 1], near_in.at[p, 0, 1], (n_send, n_recv), (p, 1), cross[p](1), tp).start()
        sums[p, 4] = Send(near_out.at[p, 1, 0], near_in.at[p, 1, 0], (n_send, n_recv), (p, 2), cross[p](-1), tp).start()
    for p in range(2):
        acc[p, ring(cross_spot[p], 1), top, :] = total(p, 1, top)
        acc[p, ring(cross_spot[p], -1), bottom, :] = total(p, -1, bottom)
    for p in range(2):
        sums[p, 0].arrived()
        near_out[p, 0, 0] = (acc[p, ring(cross_spot[p], 1), top, :] + far_in[p, 0].astype(F32)).astype(BF16)
        sums[p, 2] = Send(near_out.at[p, 0, 0], near_in.at[p, 0, 0], (n_send, n_recv), (p, 0), cross[p](1), tp).start()
        sums[p, 1].arrived()
        near_out[p, 1, 1] = (acc[p, ring(cross_spot[p], -1), bottom, :] + far_in[p, 1].astype(F32)).astype(BF16)
        sums[p, 5] = Send(near_out.at[p, 1, 1], near_in.at[p, 1, 1], (n_send, n_recv), (p, 3), cross[p](-1), tp).start()
    for p in range(2):
        for half, span in enumerate((top, bottom)):
            acc[p, cross_spot[p], span, :] = total(p, 0, span)
    for p, out in enumerate((kw_out, vw_out)):
        for half in (0, 1):
            for i in ((2, 4), (3, 5))[half]:
                sums[p, i].arrived()
            span = pl.ds(512 * half, 512)
            value = (acc[p, cross_spot[p], span, :] + near_in[p, 0, half].astype(F32)) + near_in[p, 1, half].astype(F32)
            out[:, 512 * half:512 * half + 512] = value.T.astype(BF16)

    for group in routes:
        for route in group:
            route.left()
    for group in gather:
        for send in group.values():
            send.left()
    for group in (spread, second, shared, passed, sums):
        for send in group.values():
            send.left()


def shards(queries, states, state_doc, state_pos, lengths, offsets, key_weight, value_weight, context_grad):
    docs = lax.axis_size("seq")
    parts = lax.axis_size("tp")
    rows, features = states.shape
    count, width = queries.shape
    any_spec = pl.BlockSpec(memory_space=pl.ANY)
    vmem_spec = pl.BlockSpec(memory_space=pltpu.VMEM)
    smem_spec = pl.BlockSpec(memory_space=pltpu.SMEM)
    dma = pltpu.SemaphoreType.DMA
    pair = lambda *shape: [dma(shape), dma(shape)]
    return pl.pallas_call(
        functools.partial(kernel, docs),
        out_shape=[jax.ShapeDtypeStruct((count, width), BF16), jax.ShapeDtypeStruct((256, width), BF16),
                   jax.ShapeDtypeStruct((256, width), BF16)],
        in_specs=[vmem_spec, vmem_spec, smem_spec, smem_spec] + [any_spec] * 5,
        out_specs=[vmem_spec] * 3,
        scratch_shapes=[
            pltpu.VMEM((rows, features), BF16),
            pltpu.VMEM((count, width), BF16),
            pltpu.VMEM((count, width), BF16),
            pltpu.VMEM((WSLOTS, 2, features, width), BF16),
            pltpu.VMEM((2, docs, SLOTS, 256), BF16),
            pltpu.VMEM((2, docs, SLOTS, 256), BF16),
            pltpu.VMEM((16, rows, 256), BF16),
            pltpu.VMEM((2, 4, width, 256), F32),
            pltpu.VMEM((2, rows, width), BF16),
            pltpu.VMEM((2, width, rows), BF16),
            pltpu.VMEM((2, 3, width, rows), BF16),
            pltpu.VMEM((2, 3, 4, rows, 256), BF16),
            pltpu.VMEM((2, 2, 512, 256), BF16),
            pltpu.VMEM((2, 2, 512, 256), BF16),
            pltpu.VMEM((2, 2, 2, 512, 256), BF16),
            pltpu.VMEM((2, 2, 2, 512, 256), BF16),
            dma((3,)), dma((WSLOTS, 2)),
            *pair(2, docs), *pair(2, 7), *pair(2, 3), *pair(2, 8),
            *pair(2, 4, 2), *pair(2, 4), *pair(2, 2), *pair(2, 4),
        ],
        compiler_params=pltpu.CompilerParams(collective_id=0, has_side_effects=True, vmem_limit_bytes=67043328),
        name="routed",
    )(state_doc.reshape(-1, 128), state_pos.reshape(-1, 128), lengths, offsets, queries, states,
      key_weight.reshape(parts, features, width), value_weight.reshape(parts, features, width), context_grad)


def solution(mesh):
    in_specs = (P("seq", "tp"), P("seq", "tp"), P(), P(), P(), P(), P(None, "tp"), P(None, "tp"), P("seq", "tp"))
    out_specs = (P("seq", "tp"), P("seq", "tp"), P("seq", "tp"))
    return jax.shard_map(shards, mesh=mesh, in_specs=in_specs, out_specs=out_specs, check_vma=False)
```

```python
import functools

import jax
import jax.numpy as jnp
from jax import lax
from jax.experimental import pallas as pl
from jax.experimental.pallas import tpu as pltpu
from jax.sharding import PartitionSpec as P

HEAD_DIM = 128
SLOTS = 64
F32 = jnp.float32
BF16 = jnp.bfloat16


def dot_nt(a, b):
    return lax.dot_general(a, b, (((1,), (1,)), ((), ())), preferred_element_type=F32)


def dot_tn(a, b):
    return lax.dot_general(a, b, (((0,), (0,)), ((), ())), preferred_element_type=F32)


def strict_upper(n):
    return (lax.broadcasted_iota(jnp.int32, (n, n), 0) < lax.broadcasted_iota(jnp.int32, (n, n), 1)).astype(F32).astype(BF16)


def pack_table(doc_ref, me, docs, rows):
    own = jnp.concatenate([doc_ref[pl.ds(4 * me + j, 1), :] for j in range(4)], axis=1)
    member = lax.broadcasted_iota(jnp.int32, (docs, rows), 0) == own
    member_f = member.astype(F32)
    ranks = jnp.dot(member_f.astype(BF16), strict_upper(rows), preferred_element_type=F32)
    rank = jnp.sum(ranks * member_f, axis=0, keepdims=True).astype(jnp.int32)
    target = own * SLOTS + rank
    hot = lax.broadcasted_iota(jnp.int32, (docs * SLOTS, rows), 0) == target
    return hot.astype(F32).astype(BF16)


def order_table(doc_ref, pos_ref, me, docs, rows):
    docs_all = jnp.concatenate([doc_ref[pl.ds(j, docs, stride=4), :] for j in range(4)], axis=1)
    pos_all = jnp.concatenate([pos_ref[pl.ds(j, docs, stride=4), :] for j in range(4)], axis=1)
    member = docs_all == me
    member_f = member.astype(F32)
    ranks = jnp.dot(member_f.astype(BF16), strict_upper(rows), preferred_element_type=F32).astype(jnp.int32)
    ranks = jnp.where(member, ranks, -1)
    high = (pos_all // 2).astype(F32)
    low = (pos_all % 2).astype(F32)
    parts = []
    for s in range(docs):
        hot = (lax.broadcasted_iota(jnp.int32, (SLOTS, rows), 0) == ranks[s:s + 1, :]).astype(F32).astype(BF16)
        three = jnp.concatenate([high[s:s + 1], low[s:s + 1], jnp.ones((1, rows), F32), jnp.zeros((5, rows), F32)], axis=0)
        parts.append(dot_nt(three.astype(BF16), hot))
    table = jnp.concatenate(parts, axis=1)
    slot_pos = (2.0 * table[0:1] + table[1:2] + table[2:3]).astype(jnp.int32) - 1
    hot = lax.broadcasted_iota(jnp.int32, (rows, docs * SLOTS), 0) == slot_pos
    return hot.astype(F32).astype(BF16)


def attention_head(q, k, v, g, length, offset):
    scale = HEAD_DIM ** (-0.5)
    queries, rows = q.shape[0], k.shape[0]
    scores = dot_nt(q, k) * scale
    index = lax.broadcasted_iota(jnp.int32, (queries, rows), 0)
    pos = lax.broadcasted_iota(jnp.int32, (queries, rows), 1)
    visible = (pos <= index + offset) & (pos < length)
    scores = jnp.where(visible, scores, -jnp.inf)
    weights = jnp.exp(scores - jnp.max(scores, axis=1, keepdims=True))
    probs = weights * (1.0 / jnp.sum(weights, axis=1, keepdims=True))
    low = probs.astype(BF16)
    prob_grad = dot_nt(g, v)
    delta = jnp.sum(low.astype(F32) * prob_grad, axis=1, keepdims=True)
    score_grad = (probs * (prob_grad - delta) * scale).astype(BF16)
    q_grad = jnp.dot(score_grad, k, preferred_element_type=F32).astype(BF16)
    k_grad = dot_tn(q, score_grad).astype(BF16)
    v_grad = dot_tn(g, low).astype(BF16)
    return q_grad, k_grad, v_grad


MESH = pl.DeviceIdType.MESH
WSLOTS = 5
STARTED = []


class Send:
    def __init__(self, src, dst, sems, index, seq, tp):
        send, recv = sems
        self.copy = pltpu.make_async_remote_copy(
            src_ref=src, dst_ref=dst, send_sem=send.at[index], recv_sem=recv.at[index],
            device_id={"seq": seq, "tp": tp}, device_id_type=MESH)
        self.waited = False

    def start(self):
        self.copy.start()
        STARTED.append(self)
        return self

    def arrived(self):
        self.copy.wait_recv()
        self.waited = True

    def finish(self):
        if not self.waited:
            self.arrived()
        self.copy.wait_send()


def kernel(docs, doc_ref, pos_ref, len_ref, off_ref, q_hbm, s_hbm, wk_hbm, wv_hbm, g_hbm,
           qg_out, kw_out, vw_out,
           states, queries, grads, weights, packed, arrived, own, acc, kv, gown, gfar, sfar,
           far_out, far_in, near_out, near_in,
           load_sem, w_sem, a_send, a_recv, b_send, b_recv, c_send, c_recv, d_send, d_recv,
           g_send, g_recv, f_send, f_recv, r_send, r_recv, n_send, n_recv):
    STARTED.clear()

    def drain():
        for send in STARTED:
            send.finish()

    rows = states.shape[0]
    me, tp = lax.axis_index("seq"), lax.axis_index("tp")
    x, z = me // 4, me % 4
    y, core = tp // 2, tp % 2

    def ring(v, k):
        return (v + k % 4) % 4

    def at_x(k):
        return ring(x, k) * 4 + z

    def at_z(k):
        return x * 4 + ring(z, k)

    def at_y(k, c=None):
        return ring(y, k) * 2 + (core if c is None else c)

    other = 1 - core
    partner = y * 2 + other
    line = (at_x, at_z)
    cross = (at_z, at_x)
    spot = (x, z)
    cross_spot = (z, x)

    loads = [pltpu.make_async_copy(s, d, load_sem.at[i])
             for i, (s, d) in enumerate(((s_hbm, states), (q_hbm, queries), (g_hbm, grads)))]
    for load in loads:
        load.start()
    slices = [at_y(0), partner, at_y(-1), at_y(1), at_y(-1, other), at_y(1, other), at_y(2), at_y(2, other)]

    def weight_loads(i):
        slot = i % WSLOTS
        return [pltpu.make_async_copy(w.at[slices[i]], weights.at[slot, p], w_sem.at[slot, p])
                for p, w in enumerate((wk_hbm, wv_hbm))]

    for i in range(WSLOTS):
        for load in weight_loads(i):
            load.start()

    barrier = pltpu.get_barrier_semaphore()
    for k in range(1, docs):
        pl.semaphore_signal(barrier, inc=1, device_id={"seq": (me + k) % docs, "tp": tp}, device_id_type=MESH)
    for t in (at_y(1), at_y(-1), partner):
        pl.semaphore_signal(barrier, inc=1, device_id={"seq": me, "tp": t}, device_id_type=MESH)

    table = pack_table(doc_ref, me, docs, rows)
    loads[0].wait()
    for h in range(2):
        block = jnp.dot(table, states[:, 256 * h:256 * h + 256], preferred_element_type=F32).astype(BF16)
        packed[h] = block.reshape(docs, SLOTS, 256)
    pl.semaphore_wait(barrier, docs - 1 + 3)
    routes = [[], []]
    for h in range(2):
        for k in range(1, docs):
            to = (me + k) % docs
            routes[h].append(Send(packed.at[h, to], arrived.at[h, me], (a_send, a_recv), (h, k), to, tp).start())
        arrived[h, me] = packed[h, me]
    table = order_table(doc_ref, pos_ref, me, docs, rows)

    gather = [{}, {}]
    for h in range(2):
        for route in routes[h]:
            route.arrived()
        own[2 * tp + h] = jnp.dot(table, arrived[h].reshape(docs * SLOTS, 256), preferred_element_type=F32).astype(BF16)
        piece = own.at[2 * tp + h]
        for i, t in enumerate((at_y(1), at_y(-1), partner)):
            gather[h][i] = Send(piece, piece, (b_send, b_recv), (h, i), me, t).start()

    def pass_on(h, i, origin, to):
        piece = own.at[2 * origin + h]
        gather[h][i] = Send(piece, piece, (b_send, b_recv), (h, i), me, to).start()

    def project(i):
        for load in weight_loads(i):
            load.wait()
        slot, part = i % WSLOTS, slices[i]
        last = i == len(slices) - 1

        def step(n, carry):
            left = jnp.concatenate([own[2 * part], own[2 * part + 1]], axis=1)
            p, m = n // (1024 // 1024), n % (1024 // 1024)
            cols = pl.ds(pl.multiple_of(m * 1024, 1024), 1024)
            value = jnp.dot(left, weights[slot, p, :, cols], preferred_element_type=F32)
            for b in range(1024 // 256):
                j = m * (1024 // 256) + b
                v = value[:, 256 * b:256 * b + 256]
                if i > 0:
                    v = acc[p, j, :rows, :] + v
                if last:
                    kv[p, :, pl.ds(pl.multiple_of(j * 256, 256), 256)] = v.astype(BF16)
                else:
                    acc[p, j, :rows, :] = v
            return carry

        lax.fori_loop(0, 2, step, 0)
        if i + WSLOTS < len(slices):
            for load in weight_loads(i + WSLOTS):
                load.start()

    project(0)
    for h in range(2):
        gather[h][2].arrived()
    project(1)
    gather[0][0].arrived()
    pass_on(0, 3, at_y(-1), at_y(1))
    pass_on(0, 4, at_y(-1), partner)
    gather[0][1].arrived()
    pass_on(0, 5, at_y(1), partner)
    gather[1][1].arrived()
    pass_on(1, 3, at_y(1), at_y(-1))
    pass_on(1, 5, at_y(1), partner)
    gather[1][0].arrived()
    pass_on(1, 4, at_y(-1), partner)
    project(2)
    project(3)
    for h in range(2):
        gather[h][4].arrived()
        gather[h][5].arrived()
    project(4)
    for h in range(2):
        gather[h][3].arrived()
        pass_on(h, 6, at_y(2), partner)
    project(5)
    for h in range(2):
        gather[h][6].arrived()

    mine = pl.ds(pl.multiple_of(tp * 64, 64), 64)

    view = own.reshape(4, 4, rows, 256)

    def wanted(p, k, span):
        return view.at[ring(x, k), :, span, :] if p == 0 else view.at[:, ring(z, k), span, :]

    spread = {}
    for p in range(2):
        for slot, k in ((0, 1), (2, -1), (1, 2)):
            spread[p, slot] = Send(wanted(p, k, mine), sfar.at[p, slot, :, mine, :], (c_send, c_recv), (p, slot),
                                   line[p](k), tp).start()
    project(6)
    project(7)
    for load in loads[1:]:
        load.wait()

    second = {}

    def part_of(p, origin, js=None):
        span = pl.ds(pl.multiple_of(origin * 64, 64), 64)
        return sfar.at[p, :, :, span, :] if js is None else sfar.at[p, :, js, span, :]

    def hand(p, i, origin, to, js=None):
        piece = part_of(p, origin, js)
        second[p, i] = Send(piece, piece, (d_send, d_recv), (p, i), me, to).start()

    def second_own(p):
        for slot in range(3):
            spread[p, slot].arrived()
        for i, t in enumerate((at_y(1), at_y(-1), partner)):
            hand(p, i, tp, t)

    def second_near(p):
        second[p, 0].arrived()
        hand(p, 3, at_y(-1), at_y(1), pl.ds(0, 2))
        hand(p, 4, at_y(-1), partner)
        second[p, 1].arrived()
        hand(p, 7, at_y(1), at_y(-1), pl.ds(2, 2))
        hand(p, 5, at_y(1), partner)

    def second_far(p):
        second[p, 3].arrived()
        second[p, 7].arrived()
        hand(p, 6, at_y(2), partner)

    def second_all(p):
        for i in (2, 4, 5, 6):
            second[p, i].arrived()

    length, offset = len_ref[me], off_ref[me]
    shared = {}
    for chunk in range(4):
        def head(i, carry):
            at = pl.multiple_of((2 * chunk + i) * HEAD_DIM, HEAD_DIM)
            cols = pl.ds(at, HEAD_DIM)
            qg, kg, vg = attention_head(queries[:, cols], kv[0, :, cols], kv[1, :, cols], grads[:, cols], length, offset)
            qg_out[:, cols] = qg
            gown[0, cols, :] = kg
            gown[1, cols, :] = vg
            return carry

        lax.fori_loop(0, 2, head, 0)
        span = pl.ds(256 * chunk, 256)
        for p in range(2):
            for side, (k, slot) in enumerate(((1, 0), (-1, 2))):
                shared[p, chunk, side] = Send(gown.at[p, span, :], gfar.at[p, slot, span, :], (g_send, g_recv),
                                              (p, chunk, side), line[p](k), tp).start()
        if chunk == 0:
            second_own(0)
            second_own(1)

    passed = {}

    def forward(p, chunk):
        side = 0 if chunk < 2 else 1
        k, slot = ((1, 0), (-1, 2))[side]
        span = pl.ds(256 * chunk, 256)
        shared[p, chunk, side].arrived()
        passed[p, chunk] = Send(gfar.at[p, slot, span, :], gfar.at[p, 1, span, :], (f_send, f_recv), (p, chunk),
                                line[p](k), tp).start()

    def multiply(p, grad, state, first=False):
        def step(j, carry):
            value = jnp.dot(grad[...], state(j), preferred_element_type=F32)
            acc[p, j] = value if first else acc[p, j] + value
            return carry

        lax.fori_loop(0, 4, step, 0)

    def mine_for(p):
        return (lambda j: own[4 * x + j]) if p == 0 else (lambda j: own[4 * j + z])

    def theirs(p, slot):
        return lambda j: sfar[p, slot, j]

    def near_docs(p):
        for side, slot in ((0, 0), (1, 2)):
            for chunk in range(4):
                if (chunk < 2) != (side == 0):
                    shared[p, chunk, side].arrived()
            multiply(p, gfar.at[p, slot], theirs(p, slot))

    multiply(0, gown.at[0], mine_for(0), True)
    second_near(0)
    multiply(1, gown.at[1], mine_for(1), True)
    for p in range(2):
        forward(p, 0)
        forward(p, 1)
    second_near(1)
    for p in range(2):
        forward(p, 2)
        forward(p, 3)
    second_far(0)
    second_all(0)
    near_docs(0)
    second_far(1)
    second_all(1)
    near_docs(1)

    top, bottom = pl.ds(0, 512), pl.ds(512, 512)

    def total(p, k, span):
        j = ring(cross_spot[p], k)
        return acc[p, j, span, :] + jnp.dot(gfar[p, 1, span, :], sfar[p, 1, j], preferred_element_type=F32)

    sums = {}

    def give(p, i, src, dst, k, sems):
        sums[p, i] = Send(src, dst, sems, (p, i), cross[p](k), tp).start()

    for p in range(2):
        for chunk in range(4):
            passed[p, chunk].arrived()
        far_out[p, 0] = total(p, 2, top).astype(BF16)
        far_out[p, 1] = total(p, 2, bottom).astype(BF16)
        give(p, 0, far_out.at[p, 0], far_in.at[p, 0], 1, (r_send, r_recv))
        give(p, 1, far_out.at[p, 1], far_in.at[p, 1], -1, (r_send, r_recv))
    for p in range(2):
        near_out[p, 0, 1] = total(p, 1, bottom).astype(BF16)
        near_out[p, 1, 0] = total(p, -1, top).astype(BF16)
        sums[p, 3] = Send(near_out.at[p, 0, 1], near_in.at[p, 0, 1], (n_send, n_recv), (p, 1), cross[p](1), tp).start()
        sums[p, 4] = Send(near_out.at[p, 1, 0], near_in.at[p, 1, 0], (n_send, n_recv), (p, 2), cross[p](-1), tp).start()
    for p in range(2):
        acc[p, ring(cross_spot[p], 1), top, :] = total(p, 1, top)
        acc[p, ring(cross_spot[p], -1), bottom, :] = total(p, -1, bottom)
    for p in range(2):
        sums[p, 0].arrived()
        near_out[p, 0, 0] = (acc[p, ring(cross_spot[p], 1), top, :] + far_in[p, 0].astype(F32)).astype(BF16)
        sums[p, 2] = Send(near_out.at[p, 0, 0], near_in.at[p, 0, 0], (n_send, n_recv), (p, 0), cross[p](1), tp).start()
        sums[p, 1].arrived()
        near_out[p, 1, 1] = (acc[p, ring(cross_spot[p], -1), bottom, :] + far_in[p, 1].astype(F32)).astype(BF16)
        sums[p, 5] = Send(near_out.at[p, 1, 1], near_in.at[p, 1, 1], (n_send, n_recv), (p, 3), cross[p](-1), tp).start()
    for p in range(2):
        for half, span in enumerate((top, bottom)):
            acc[p, cross_spot[p], span, :] = total(p, 0, span)
    for p, out in enumerate((kw_out, vw_out)):
        for half in (0, 1):
            for i in ((2, 4), (3, 5))[half]:
                sums[p, i].arrived()
            span = pl.ds(512 * half, 512)
            value = (acc[p, cross_spot[p], span, :] + near_in[p, 0, half].astype(F32)) + near_in[p, 1, half].astype(F32)
            out[:, 512 * half:512 * half + 512] = value.T.astype(BF16)

    drain()


def hand_over(*refs):
    for source, target in zip(refs[:3], refs[3:]):
        target[...] = source[...]


def shards(queries, states, state_doc, state_pos, lengths, offsets, key_weight, value_weight, context_grad):
    docs = lax.axis_size("seq")
    parts = lax.axis_size("tp")
    rows, features = states.shape
    count, width = queries.shape
    any_spec = pl.BlockSpec(memory_space=pl.ANY)
    vmem_spec = pl.BlockSpec(memory_space=pltpu.VMEM)
    smem_spec = pl.BlockSpec(memory_space=pltpu.SMEM)
    dma = pltpu.SemaphoreType.DMA
    pair = lambda *shape: [dma(shape), dma(shape)]
    results = pl.pallas_call(
        functools.partial(kernel, docs),
        out_shape=[jax.ShapeDtypeStruct((count, width), BF16), jax.ShapeDtypeStruct((256, width), BF16),
                   jax.ShapeDtypeStruct((256, width), BF16)],
        in_specs=[vmem_spec, vmem_spec, smem_spec, smem_spec] + [any_spec] * 5,
        out_specs=[vmem_spec] * 3,
        scratch_shapes=[
            pltpu.VMEM((rows, features), BF16),
            pltpu.VMEM((count, width), BF16),
            pltpu.VMEM((count, width), BF16),
            pltpu.VMEM((WSLOTS, 2, features, width), BF16),
            pltpu.VMEM((2, docs, SLOTS, 256), BF16),
            pltpu.VMEM((2, docs, SLOTS, 256), BF16),
            pltpu.VMEM((16, rows, 256), BF16),
            pltpu.VMEM((2, 4, width, 256), F32),
            pltpu.VMEM((2, rows, width), BF16),
            pltpu.VMEM((2, width, rows), BF16),
            pltpu.VMEM((2, 3, width, rows), BF16),
            pltpu.VMEM((2, 3, 4, rows, 256), BF16),
            pltpu.VMEM((2, 2, 512, 256), BF16),
            pltpu.VMEM((2, 2, 512, 256), BF16),
            pltpu.VMEM((2, 2, 2, 512, 256), BF16),
            pltpu.VMEM((2, 2, 2, 512, 256), BF16),
            dma((3,)), dma((WSLOTS, 2)),
            *pair(2, docs), *pair(2, 7), *pair(2, 3), *pair(2, 8),
            *pair(2, 4, 2), *pair(2, 4), *pair(2, 2), *pair(2, 4),
        ],
        compiler_params=pltpu.CompilerParams(collective_id=0, has_side_effects=True, vmem_limit_bytes=67043328),
        name="routed",
    )(state_doc.reshape(-1, 128), state_pos.reshape(-1, 128), lengths, offsets, queries, states,
      key_weight.reshape(parts, features, width), value_weight.reshape(parts, features, width), context_grad)
    block = pl.BlockSpec((64, width), lambda i: (i, 0))
    return pl.pallas_call(
        hand_over,
        grid=(4,),
        out_shape=[jax.ShapeDtypeStruct((256, width), BF16)] * 3,
        in_specs=[block] * 3,
        out_specs=[block] * 3,
        name="hand_over",
    )(*results)


def solution(mesh):
    in_specs = (P("seq", "tp"), P("seq", "tp"), P(), P(), P(), P(), P(None, "tp"), P(None, "tp"), P("seq", "tp"))
    out_specs = (P("seq", "tp"), P("seq", "tp"), P("seq", "tp"))
    return jax.shard_map(shards, mesh=mesh, in_specs=in_specs, out_specs=out_specs, check_vma=False)
```

```python
import functools

import jax
import jax.numpy as jnp
from jax import lax
from jax.experimental import pallas as pl
from jax.experimental.pallas import tpu as pltpu
from jax.sharding import PartitionSpec as P

HEAD_DIM = 128
SLOTS = 64
USED = 56
F32 = jnp.float32
BF16 = jnp.bfloat16


def dot_nt(a, b):
    return lax.dot_general(a, b, (((1,), (1,)), ((), ())), preferred_element_type=F32)


def dot_tn(a, b):
    return lax.dot_general(a, b, (((0,), (0,)), ((), ())), preferred_element_type=F32)


def strict_upper(n):
    return (lax.broadcasted_iota(jnp.int32, (n, n), 0) < lax.broadcasted_iota(jnp.int32, (n, n), 1)).astype(F32).astype(BF16)


def pack_table(doc_ref, me, docs, rows):
    own = jnp.concatenate([doc_ref[pl.ds(4 * me + j, 1), :] for j in range(4)], axis=1)
    member = lax.broadcasted_iota(jnp.int32, (docs, rows), 0) == own
    member_f = member.astype(F32)
    ranks = jnp.dot(member_f.astype(BF16), strict_upper(rows), preferred_element_type=F32)
    rank = jnp.sum(ranks * member_f, axis=0, keepdims=True).astype(jnp.int32)
    target = own * SLOTS + rank
    hot = lax.broadcasted_iota(jnp.int32, (docs * SLOTS, rows), 0) == target
    return hot.astype(F32).astype(BF16)


def order_table(doc_ref, pos_ref, me, docs, rows):
    docs_all = jnp.concatenate([doc_ref[pl.ds(j, docs, stride=4), :] for j in range(4)], axis=1)
    pos_all = jnp.concatenate([pos_ref[pl.ds(j, docs, stride=4), :] for j in range(4)], axis=1)
    member = docs_all == me
    member_f = member.astype(F32)
    ranks = jnp.dot(member_f.astype(BF16), strict_upper(rows), preferred_element_type=F32).astype(jnp.int32)
    ranks = jnp.where(member, ranks, -1)
    high = (pos_all // 2).astype(F32)
    low = (pos_all % 2).astype(F32)
    parts = []
    for s in range(docs):
        hot = (lax.broadcasted_iota(jnp.int32, (SLOTS, rows), 0) == ranks[s:s + 1, :]).astype(F32).astype(BF16)
        three = jnp.concatenate([high[s:s + 1], low[s:s + 1], jnp.ones((1, rows), F32), jnp.zeros((5, rows), F32)], axis=0)
        parts.append(dot_nt(three.astype(BF16), hot))
    table = jnp.concatenate(parts, axis=1)
    slot_pos = (2.0 * table[0:1] + table[1:2] + table[2:3]).astype(jnp.int32) - 1
    hot = lax.broadcasted_iota(jnp.int32, (rows, docs * SLOTS), 0) == slot_pos
    return hot.astype(F32).astype(BF16)


def attention_head(q, k, v, g, length, offset):
    scale = HEAD_DIM ** (-0.5)
    queries, rows = q.shape[0], k.shape[0]
    scores = dot_nt(q, k) * scale
    index = lax.broadcasted_iota(jnp.int32, (queries, rows), 0)
    pos = lax.broadcasted_iota(jnp.int32, (queries, rows), 1)
    visible = (pos <= index + offset) & (pos < length)
    scores = jnp.where(visible, scores, -jnp.inf)
    weights = jnp.exp(scores - jnp.max(scores, axis=1, keepdims=True))
    probs = weights * (1.0 / jnp.sum(weights, axis=1, keepdims=True))
    low = probs.astype(BF16)
    prob_grad = dot_nt(g, v)
    delta = jnp.sum(low.astype(F32) * prob_grad, axis=1, keepdims=True)
    score_grad = (probs * (prob_grad - delta) * scale).astype(BF16)
    q_grad = jnp.dot(score_grad, k, preferred_element_type=F32).astype(BF16)
    k_grad = dot_tn(q, score_grad).astype(BF16)
    v_grad = dot_tn(g, low).astype(BF16)
    return q_grad, k_grad, v_grad


MESH = pl.DeviceIdType.MESH
WSLOTS = 5
STARTED = []


class Send:
    def __init__(self, src, dst, sems, index, seq, tp):
        send, recv = sems
        self.copy = pltpu.make_async_remote_copy(
            src_ref=src, dst_ref=dst, send_sem=send.at[index], recv_sem=recv.at[index],
            device_id={"seq": seq, "tp": tp}, device_id_type=MESH)
        self.waited = False

    def start(self):
        self.copy.start()
        STARTED.append(self)
        return self

    def arrived(self):
        self.copy.wait_recv()
        self.waited = True

    def finish(self):
        if not self.waited:
            self.arrived()
        self.copy.wait_send()


def kernel(docs, doc_ref, pos_ref, len_ref, off_ref, q_hbm, s_hbm, wk_hbm, wv_hbm, g_hbm,
           qg_out, kw_out, vw_out,
           states, queries, grads, weights, packed, arrived, own, acc, kv, gown, gfar, sfar,
           far_out, far_in, near_out, near_in,
           load_sem, w_sem, a_send, a_recv, b_send, b_recv, c_send, c_recv, d_send, d_recv,
           g_send, g_recv, f_send, f_recv, r_send, r_recv, n_send, n_recv):
    STARTED.clear()

    def drain():
        for send in STARTED:
            send.finish()

    rows = states.shape[0]
    me, tp = lax.axis_index("seq"), lax.axis_index("tp")
    x, z = me // 4, me % 4
    y, core = tp // 2, tp % 2

    def ring(v, k):
        return (v + k % 4) % 4

    def at_x(k):
        return ring(x, k) * 4 + z

    def at_z(k):
        return x * 4 + ring(z, k)

    def at_y(k, c=None):
        return ring(y, k) * 2 + (core if c is None else c)

    other = 1 - core
    partner = y * 2 + other
    line = (at_x, at_z)
    cross = (at_z, at_x)
    spot = (x, z)
    cross_spot = (z, x)

    loads = [pltpu.make_async_copy(s, d, load_sem.at[i])
             for i, (s, d) in enumerate(((s_hbm, states), (q_hbm, queries), (g_hbm, grads)))]
    for load in loads:
        load.start()
    slices = [at_y(0), partner, at_y(-1), at_y(1), at_y(-1, other), at_y(1, other), at_y(2, 0), at_y(2, 1)]

    def weight_loads(i):
        slot = i % WSLOTS
        return [pltpu.make_async_copy(w.at[slices[i]], weights.at[slot, p], w_sem.at[slot, p])
                for p, w in enumerate((wk_hbm, wv_hbm))]

    for i in range(WSLOTS):
        for load in weight_loads(i):
            load.start()

    arrived[:, :, 48:, :] = jnp.zeros((4, docs, SLOTS - 48, 128), BF16)

    barrier = pltpu.get_barrier_semaphore()
    for k in range(1, docs):
        pl.semaphore_signal(barrier, inc=1, device_id={"seq": (me + k) % docs, "tp": tp}, device_id_type=MESH)
    for t in (at_y(1), at_y(-1), partner):
        pl.semaphore_signal(barrier, inc=1, device_id={"seq": me, "tp": t}, device_id_type=MESH)

    table = pack_table(doc_ref, me, docs, rows)
    loads[0].wait()
    for h in range(2):
        block = jnp.dot(table, states[:, 256 * h:256 * h + 256], preferred_element_type=F32).astype(BF16)
        packed[2 * h] = block[:, :128].reshape(docs, SLOTS, 128)
        packed[2 * h + 1] = block[:, 128:].reshape(docs, SLOTS, 128)
    pl.semaphore_wait(barrier, docs - 1 + 3)
    routes = [[], [], [], []]
    for q in range(4):
        for k in range(1, docs):
            to = (me + k) % docs
            routes[q].append(Send(packed.at[q, to, pl.ds(0, USED)], arrived.at[q, me, pl.ds(0, USED)], (a_send, a_recv),
                                  (q, k), to, tp).start())
        arrived[q, me] = packed[q, me]
    table = order_table(doc_ref, pos_ref, me, docs, rows)

    gather = [{}, {}, {}, {}]

    def pass_on(q, i, origin, to):
        piece = own.at[2 * origin + q // 2, :, pl.ds(128 * (q % 2), 128)]
        gather[q][i] = Send(piece, piece, (b_send, b_recv), (q, i), me, to).start()

    for q in range(4):
        for route in routes[q]:
            route.arrived()
        value = jnp.dot(table, arrived[q].reshape(docs * SLOTS, 128), preferred_element_type=F32)
        own[2 * tp + q // 2, :, 128 * (q % 2):128 * (q % 2) + 128] = value.astype(BF16)
        for i, t in enumerate((at_y(1), at_y(-1), partner)):
            pass_on(q, i, tp, t)

    mine = pl.ds(pl.multiple_of(tp * 64, 64), 64)

    def line_copy(p, k, src, js, to):
        return pltpu.make_async_remote_copy(
            src_ref=src, dst_ref=sfar.at[p, k - 1, js, mine, :], send_sem=c_send.at[p, k - 1], recv_sem=c_recv.at[p, k - 1],
            device_id={"seq": to, "tp": tp}, device_id_type=MESH)

    def spread(part):
        k = (part // 2 + 4 - x) % 4

        @pl.when(k != 0)
        def _():
            line_copy(0, k, own.at[pl.ds(2 * part, 2), mine, :], pl.ds(2 * (part % 2), 2), (part // 2) * 4 + z).start()

        for h in range(2):
            block = 2 * part + h
            l = (block % 4 + 4 - z) % 4

            @pl.when(l != 0)
            def _(block=block, l=l):
                line_copy(1, l, own.at[pl.ds(block, 1), mine, :], pl.ds(block // 4, 1), x * 4 + block % 4).start()

    def spread_all(p, slot):
        to = line[p](slot + 1)
        return line_copy(p, slot + 1, sfar.at[p, slot, :, mine, :], slice(None), to)

    def project(i):
        for load in weight_loads(i):
            load.wait()
        slot, part = i % WSLOTS, slices[i]

        def step(n, carry):
            left = jnp.concatenate([own[2 * part], own[2 * part + 1]], axis=1)
            p, m = n // (1024 // 1024), n % (1024 // 1024)
            cols = pl.ds(pl.multiple_of(m * 1024, 1024), 1024)
            value = jnp.dot(left, weights[slot, p, :, cols], preferred_element_type=F32)
            for b in range(1024 // 256):
                j = m * (1024 // 256) + b
                v = value[:, 256 * b:256 * b + 256]
                if i > 0:
                    v = acc[p, j, :rows, :] + v
                acc[p, j, :rows, :] = v
            return carry

        lax.fori_loop(0, 2, step, 0)
        if i + WSLOTS < len(slices):
            for load in weight_loads(i + WSLOTS):
                load.start()

    spread(tp)
    project(0)
    for q in range(4):
        gather[q][2].arrived()
    spread(partner)
    project(1)
    for q in range(4):
        gather[q][0].arrived()
        if q < 2:
            pass_on(q, 3, at_y(-1), at_y(1))
        pass_on(q, 4, at_y(-1), partner)
        gather[q][1].arrived()
        if q >= 2:
            pass_on(q, 3, at_y(1), at_y(-1))
        pass_on(q, 5, at_y(1), partner)
    spread(at_y(-1))
    spread(at_y(1))
    project(2)
    project(3)
    for q in range(4):
        gather[q][4].arrived()
        gather[q][5].arrived()
    spread(at_y(-1, other))
    spread(at_y(1, other))
    project(4)
    for q in range(4):
        gather[q][3].arrived()
        pass_on(q, 6, at_y(2), partner)
    spread(at_y(2))
    project(5)
    for q in range(4):
        gather[q][6].arrived()
    spread(at_y(2, other))
    for load in loads[1:]:
        load.wait()
    for i in (6, 7):
        for load in weight_loads(i):
            load.wait()

    second = {}

    def part_of(p, origin, js=None):
        span = pl.ds(pl.multiple_of(origin * 64, 64), 64)
        return sfar.at[p, :, :, span, :] if js is None else sfar.at[p, :, js, span, :]

    def hand(p, i, origin, to, js=None):
        piece = part_of(p, origin, js)
        second[p, i] = Send(piece, piece, (d_send, d_recv), (p, i), me, to).start()

    def second_own(p):
        for slot in range(3):
            spread_all(p, slot).wait_recv()
        for i, t in enumerate((at_y(1), at_y(-1), partner)):
            hand(p, i, tp, t)

    def second_near(p):
        second[p, 0].arrived()
        hand(p, 3, at_y(-1), at_y(1), pl.ds(0, 2))
        hand(p, 4, at_y(-1), partner)
        second[p, 1].arrived()
        hand(p, 7, at_y(1), at_y(-1), pl.ds(2, 2))
        hand(p, 5, at_y(1), partner)

    def second_far(p):
        second[p, 3].arrived()
        second[p, 7].arrived()
        hand(p, 6, at_y(2), partner)

    def second_all(p):
        for i in (2, 4, 5, 6):
            second[p, i].arrived()

    length, offset = len_ref[me], off_ref[me]
    shared = {}
    view = own.reshape(4, 4, rows, 256)
    for chunk in range(4):
        last = jnp.concatenate([view[ring(y, 2), b] for b in range(4)], axis=1)
        for p in range(2):
            part = weights[6 - WSLOTS:8 - WSLOTS, p, :, 256 * chunk:256 * chunk + 256].reshape(4 * 256, 256)
            value = acc[p, chunk, :rows, :] + jnp.dot(last, part, preferred_element_type=F32)
            kv[p, :, 256 * chunk:256 * chunk + 256] = value.astype(BF16)

        def head(i, carry):
            at = pl.multiple_of((2 * chunk + i) * HEAD_DIM, HEAD_DIM)
            cols = pl.ds(at, HEAD_DIM)
            qg, kg, vg = attention_head(queries[:, cols], kv[0, :, cols], kv[1, :, cols], grads[:, cols], length, offset)
            qg_out[:, cols] = qg
            gown[0, cols, :] = kg
            gown[1, cols, :] = vg
            return carry

        lax.fori_loop(0, 2, head, 0)
        span = pl.ds(256 * chunk, 256)
        for p in range(2):
            for side, (k, slot) in enumerate(((1, 0), (-1, 2))):
                shared[p, chunk, side] = Send(gown.at[p, span, :], gfar.at[p, slot, span, :], (g_send, g_recv),
                                              (p, chunk, side), line[p](k), tp).start()
        if chunk == 0:
            second_own(0)
            second_own(1)


    passed = {}

    def forward(p, chunk):
        side = 0 if chunk < 2 else 1
        k, slot = ((1, 0), (-1, 2))[side]
        span = pl.ds(256 * chunk, 256)
        shared[p, chunk, side].arrived()
        passed[p, chunk] = Send(gfar.at[p, slot, span, :], gfar.at[p, 1, span, :], (f_send, f_recv), (p, chunk),
                                line[p](k), tp).start()

    def multiply(p, grad, state, first=False):
        def step(j, carry):
            value = jnp.dot(grad[...], state(j), preferred_element_type=F32)
            acc[p, j] = value if first else acc[p, j] + value
            return carry

        lax.fori_loop(0, 4, step, 0)

    def mine_for(p):
        return (lambda j: own[4 * x + j]) if p == 0 else (lambda j: own[4 * j + z])

    def theirs(p, slot):
        return lambda j: sfar[p, slot, j]

    def near_docs(p):
        for side, slot in ((0, 0), (1, 2)):
            for chunk in range(4):
                if (chunk < 2) != (side == 0):
                    shared[p, chunk, side].arrived()
            multiply(p, gfar.at[p, slot], theirs(p, slot))

    multiply(0, gown.at[0], mine_for(0), True)
    second_near(0)
    multiply(1, gown.at[1], mine_for(1), True)
    for p in range(2):
        forward(p, 0)
        forward(p, 1)
    second_near(1)
    for p in range(2):
        forward(p, 2)
        forward(p, 3)
    second_far(0)
    second_all(0)
    near_docs(0)
    second_far(1)
    second_all(1)
    near_docs(1)


    top, bottom = pl.ds(0, 512), pl.ds(512, 512)

    def total(p, k, span):
        j = ring(cross_spot[p], k)
        return acc[p, j, span, :] + jnp.dot(gfar[p, 1, span, :], sfar[p, 1, j], preferred_element_type=F32)

    sums = {}

    def give(p, i, src, dst, k, sems):
        sums[p, i] = Send(src, dst, sems, (p, i), cross[p](k), tp).start()

    for p in range(2):
        for chunk in range(4):
            passed[p, chunk].arrived()
        far_out[p, 0] = total(p, 2, top).astype(BF16)
        far_out[p, 1] = total(p, 2, bottom).astype(BF16)
        give(p, 0, far_out.at[p, 0], far_in.at[p, 0], 1, (r_send, r_recv))
        give(p, 1, far_out.at[p, 1], far_in.at[p, 1], -1, (r_send, r_recv))
    for p in range(2):
        near_out[p, 0, 1] = total(p, 1, bottom).astype(BF16)
        near_out[p, 1, 0] = total(p, -1, top).astype(BF16)
        sums[p, 3] = Send(near_out.at[p, 0, 1], near_in.at[p, 0, 1], (n_send, n_recv), (p, 1), cross[p](1), tp).start()
        sums[p, 4] = Send(near_out.at[p, 1, 0], near_in.at[p, 1, 0], (n_send, n_recv), (p, 2), cross[p](-1), tp).start()
    for p in range(2):
        acc[p, ring(cross_spot[p], 1), top, :] = total(p, 1, top)
        acc[p, ring(cross_spot[p], -1), bottom, :] = total(p, -1, bottom)
    for p in range(2):
        sums[p, 0].arrived()
        near_out[p, 0, 0] = (acc[p, ring(cross_spot[p], 1), top, :] + far_in[p, 0].astype(F32)).astype(BF16)
        sums[p, 2] = Send(near_out.at[p, 0, 0], near_in.at[p, 0, 0], (n_send, n_recv), (p, 0), cross[p](1), tp).start()
        sums[p, 1].arrived()
        near_out[p, 1, 1] = (acc[p, ring(cross_spot[p], -1), bottom, :] + far_in[p, 1].astype(F32)).astype(BF16)
        sums[p, 5] = Send(near_out.at[p, 1, 1], near_in.at[p, 1, 1], (n_send, n_recv), (p, 3), cross[p](-1), tp).start()
    for p in range(2):
        for half, span in enumerate((top, bottom)):
            acc[p, cross_spot[p], span, :] = total(p, 0, span)
    for p, out in enumerate((kw_out, vw_out)):
        for half in (0, 1):
            for i in ((2, 4), (3, 5))[half]:
                sums[p, i].arrived()
            span = pl.ds(512 * half, 512)
            value = (acc[p, cross_spot[p], span, :] + near_in[p, 0, half].astype(F32)) + near_in[p, 1, half].astype(F32)
            out[:, 512 * half:512 * half + 512] = value.T.astype(BF16)

    for p in range(2):
        for slot in range(3):
            spread_all(p, slot).wait_send()
    drain()


def hand_over(*refs):
    copies = [pltpu.make_async_copy(refs[i], refs[3 + i], refs[6].at[i]) for i in range(3)]
    for copy in copies:
        copy.start()
    for copy in copies:
        copy.wait()


def shards(queries, states, state_doc, state_pos, lengths, offsets, key_weight, value_weight, context_grad):
    docs = lax.axis_size("seq")
    parts = lax.axis_size("tp")
    rows, features = states.shape
    count, width = queries.shape
    any_spec = pl.BlockSpec(memory_space=pl.ANY)
    vmem_spec = pl.BlockSpec(memory_space=pltpu.VMEM)
    smem_spec = pl.BlockSpec(memory_space=pltpu.SMEM)
    dma = pltpu.SemaphoreType.DMA
    pair = lambda *shape: [dma(shape), dma(shape)]
    results = pl.pallas_call(
        functools.partial(kernel, docs),
        out_shape=[pltpu.VMEM((count, width), BF16)] + [pltpu.VMEM((256, width), BF16)] * 2,
        in_specs=[vmem_spec, vmem_spec, smem_spec, smem_spec] + [any_spec] * 5,
        out_specs=[vmem_spec] * 3,
        scratch_shapes=[
            pltpu.VMEM((rows, features), BF16),
            pltpu.VMEM((count, width), BF16),
            pltpu.VMEM((count, width), BF16),
            pltpu.VMEM((WSLOTS, 2, features, width), BF16),
            pltpu.VMEM((4, docs, SLOTS, 128), BF16),
            pltpu.VMEM((4, docs, SLOTS, 128), BF16),
            pltpu.VMEM((16, rows, 256), BF16),
            pltpu.VMEM((2, 4, width, 256), F32),
            pltpu.VMEM((2, rows, width), BF16),
            pltpu.VMEM((2, width, rows), BF16),
            pltpu.VMEM((2, 3, width, rows), BF16),
            pltpu.VMEM((2, 3, 4, rows, 256), BF16),
            pltpu.VMEM((2, 2, 512, 256), BF16),
            pltpu.VMEM((2, 2, 512, 256), BF16),
            pltpu.VMEM((2, 2, 2, 512, 256), BF16),
            pltpu.VMEM((2, 2, 2, 512, 256), BF16),
            dma((3,)), dma((WSLOTS, 2)),
            *pair(4, docs), *pair(4, 7), *pair(2, 3), *pair(2, 8),
            *pair(2, 4, 2), *pair(2, 4), *pair(2, 2), *pair(2, 4),
        ],
        compiler_params=pltpu.CompilerParams(collective_id=0, has_side_effects=True, vmem_limit_bytes=60 << 20),
        name="routed",
    )(state_doc.reshape(-1, 128), state_pos.reshape(-1, 128), lengths, offsets, queries, states,
      key_weight.reshape(parts, features, width), value_weight.reshape(parts, features, width), context_grad)
    return pl.pallas_call(
        hand_over,
        out_shape=[jax.ShapeDtypeStruct((256, width), BF16)] * 3,
        in_specs=[vmem_spec] * 3,
        out_specs=[any_spec] * 3,
        scratch_shapes=[dma((3,))],
        compiler_params=pltpu.CompilerParams(vmem_limit_bytes=4 << 20),
        name="hand_over",
    )(*results)


def solution(mesh):
    in_specs = (P("seq", "tp"), P("seq", "tp"), P(), P(), P(), P(), P(None, "tp"), P(None, "tp"), P("seq", "tp"))
    out_specs = (P("seq", "tp"), P("seq", "tp"), P("seq", "tp"))
    return jax.shard_map(shards, mesh=mesh, in_specs=in_specs, out_specs=out_specs, check_vma=False)
```

```python
import functools

import jax
import jax.numpy as jnp
from jax import lax
from jax.experimental import pallas as pl
from jax.experimental.pallas import tpu as pltpu
from jax.sharding import PartitionSpec as P

HEAD_DIM = 128
SLOTS = 64
USED = 56
F32 = jnp.float32
BF16 = jnp.bfloat16


def dot_nt(a, b):
    return lax.dot_general(a, b, (((1,), (1,)), ((), ())), preferred_element_type=F32)


def dot_tn(a, b):
    return lax.dot_general(a, b, (((0,), (0,)), ((), ())), preferred_element_type=F32)


def strict_upper(n):
    return (lax.broadcasted_iota(jnp.int32, (n, n), 0) < lax.broadcasted_iota(jnp.int32, (n, n), 1)).astype(F32).astype(BF16)


def pack_table(doc_ref, me, docs, rows):
    own = jnp.concatenate([doc_ref[pl.ds(4 * me + j, 1), :] for j in range(4)], axis=1)
    member = lax.broadcasted_iota(jnp.int32, (docs, rows), 0) == own
    member_f = member.astype(F32)
    ranks = jnp.dot(member_f.astype(BF16), strict_upper(rows), preferred_element_type=F32)
    rank = jnp.sum(ranks * member_f, axis=0, keepdims=True).astype(jnp.int32)
    target = own * SLOTS + rank
    hot = lax.broadcasted_iota(jnp.int32, (docs * SLOTS, rows), 0) == target
    return hot.astype(F32).astype(BF16)


def order_table(doc_ref, pos_ref, me, docs, rows):
    docs_all = jnp.concatenate([doc_ref[pl.ds(j, docs, stride=4), :] for j in range(4)], axis=1)
    pos_all = jnp.concatenate([pos_ref[pl.ds(j, docs, stride=4), :] for j in range(4)], axis=1)
    member = docs_all == me
    member_f = member.astype(F32)
    ranks = jnp.dot(member_f.astype(BF16), strict_upper(rows), preferred_element_type=F32).astype(jnp.int32)
    ranks = jnp.where(member, ranks, -1)
    high = (pos_all // 2).astype(F32)
    low = (pos_all % 2).astype(F32)
    parts = []
    for s in range(docs):
        hot = (lax.broadcasted_iota(jnp.int32, (SLOTS, rows), 0) == ranks[s:s + 1, :]).astype(F32).astype(BF16)
        three = jnp.concatenate([high[s:s + 1], low[s:s + 1], jnp.ones((1, rows), F32), jnp.zeros((5, rows), F32)], axis=0)
        parts.append(dot_nt(three.astype(BF16), hot))
    table = jnp.concatenate(parts, axis=1)
    slot_pos = (2.0 * table[0:1] + table[1:2] + table[2:3]).astype(jnp.int32) - 1
    hot = lax.broadcasted_iota(jnp.int32, (rows, docs * SLOTS), 0) == slot_pos
    return hot.astype(F32).astype(BF16)


def attention_head(q, k, v, g, length, offset):
    scale = HEAD_DIM ** (-0.5)
    queries, rows = q.shape[0], k.shape[0]
    scores = dot_nt(q, k) * scale
    index = lax.broadcasted_iota(jnp.int32, (queries, rows), 0)
    pos = lax.broadcasted_iota(jnp.int32, (queries, rows), 1)
    visible = (pos <= index + offset) & (pos < length)
    scores = jnp.where(visible, scores, -jnp.inf)
    weights = jnp.exp(scores - jnp.max(scores, axis=1, keepdims=True))
    probs = weights * (1.0 / jnp.sum(weights, axis=1, keepdims=True))
    low = probs.astype(BF16)
    prob_grad = dot_nt(g, v)
    delta = jnp.sum(low.astype(F32) * prob_grad, axis=1, keepdims=True)
    score_grad = (probs * (prob_grad - delta) * scale).astype(BF16)
    q_grad = jnp.dot(score_grad, k, preferred_element_type=F32).astype(BF16)
    k_grad = dot_tn(q, score_grad).astype(BF16)
    v_grad = dot_tn(g, low).astype(BF16)
    return q_grad, k_grad, v_grad


MESH = pl.DeviceIdType.MESH
WSLOTS = 5
STARTED = []


class Send:
    def __init__(self, src, dst, sems, index, seq, tp):
        send, recv = sems
        self.copy = pltpu.make_async_remote_copy(
            src_ref=src, dst_ref=dst, send_sem=send.at[index], recv_sem=recv.at[index],
            device_id={"seq": seq, "tp": tp}, device_id_type=MESH)
        self.waited = False

    def start(self):
        self.copy.start()
        STARTED.append(self)
        return self

    def arrived(self):
        self.copy.wait_recv()
        self.waited = True

    def finish(self):
        if not self.waited:
            self.arrived()
        self.copy.wait_send()


def kernel(docs, doc_ref, pos_ref, len_ref, off_ref, q_hbm, s_hbm, wk_hbm, wv_hbm, g_hbm,
           qg_out, kw_out, vw_out,
           states, queries, grads, weights, packed, arrived, own, acc, kv, gown, gfar, sfar,
           far_out, far_in, near_out, near_in,
           load_sem, w_sem, a_send, a_recv, b_send, b_recv, c_send, c_recv, d_send, d_recv,
           g_send, g_recv, f_send, f_recv, r_send, r_recv, n_send, n_recv):
    STARTED.clear()

    def drain():
        for send in STARTED:
            send.finish()

    rows = states.shape[0]
    me, tp = lax.axis_index("seq"), lax.axis_index("tp")
    x, z = me // 4, me % 4
    y, core = tp // 2, tp % 2

    def ring(v, k):
        return (v + k % 4) % 4

    def at_x(k):
        return ring(x, k) * 4 + z

    def at_z(k):
        return x * 4 + ring(z, k)

    def at_y(k, c=None):
        return ring(y, k) * 2 + (core if c is None else c)

    other = 1 - core
    partner = y * 2 + other
    line = (at_x, at_z)
    cross = (at_z, at_x)
    spot = (x, z)
    cross_spot = (z, x)

    loads = [pltpu.make_async_copy(s, d, load_sem.at[i])
             for i, (s, d) in enumerate(((s_hbm, states), (q_hbm, queries), (g_hbm, grads)))]
    for load in loads:
        load.start()
    slices = [at_y(0), partner, at_y(-1), at_y(1), at_y(-1, other), at_y(1, other), at_y(2, 0), at_y(2, 1)]

    def weight_loads(i):
        slot = i % WSLOTS
        return [pltpu.make_async_copy(w.at[slices[i]], weights.at[slot, p], w_sem.at[slot, p])
                for p, w in enumerate((wk_hbm, wv_hbm))]

    for i in range(WSLOTS):
        for load in weight_loads(i):
            load.start()

    arrived[:, :, 48:, :] = jnp.zeros((4, docs, SLOTS - 48, 128), BF16)

    barrier = pltpu.get_barrier_semaphore()
    for k in range(1, docs):
        pl.semaphore_signal(barrier, inc=1, device_id={"seq": (me + k) % docs, "tp": tp}, device_id_type=MESH)
    for t in (at_y(1), at_y(-1), partner):
        pl.semaphore_signal(barrier, inc=1, device_id={"seq": me, "tp": t}, device_id_type=MESH)

    table = pack_table(doc_ref, me, docs, rows)
    loads[0].wait()
    for h in range(2):
        block = jnp.dot(table, states[:, 256 * h:256 * h + 256], preferred_element_type=F32).astype(BF16)
        packed[2 * h] = block[:, :128].reshape(docs, SLOTS, 128)
        packed[2 * h + 1] = block[:, 128:].reshape(docs, SLOTS, 128)
    pl.semaphore_wait(barrier, docs - 1 + 3)
    peers = sorted(((i, j) for i in range(4) for j in range(4) if i or j), key=lambda d: min(d[0], 4 - d[0]) + min(d[1], 4 - d[1]))
    routes = [[], [], [], []]
    for q in range(4):
        for k, (i, j) in enumerate(peers):
            to = ring(x, i) * 4 + ring(z, j)
            routes[q].append(Send(packed.at[q, to, pl.ds(0, USED)], arrived.at[q, me, pl.ds(0, USED)], (a_send, a_recv),
                                  (q, k), to, tp).start())
        arrived[q, me] = packed[q, me]
    table = order_table(doc_ref, pos_ref, me, docs, rows)

    gather = [{}, {}, {}, {}]

    def pass_on(q, i, origin, to):
        piece = own.at[2 * origin + q // 2, :, pl.ds(128 * (q % 2), 128)]
        gather[q][i] = Send(piece, piece, (b_send, b_recv), (q, i), me, to).start()

    for q in range(4):
        for route in routes[q]:
            route.arrived()
        value = jnp.dot(table, arrived[q].reshape(docs * SLOTS, 128), preferred_element_type=F32)
        own[2 * tp + q // 2, :, 128 * (q % 2):128 * (q % 2) + 128] = value.astype(BF16)
        for i, t in enumerate((at_y(1), at_y(-1), partner)):
            pass_on(q, i, tp, t)

    mine = pl.ds(pl.multiple_of(tp * 64, 64), 64)

    def line_copy(p, k, src, js, to):
        return pltpu.make_async_remote_copy(
            src_ref=src, dst_ref=sfar.at[p, k - 1, js, mine, :], send_sem=c_send.at[p, k - 1], recv_sem=c_recv.at[p, k - 1],
            device_id={"seq": to, "tp": tp}, device_id_type=MESH)

    def spread(part):
        k = (part // 2 + 4 - x) % 4

        @pl.when(k != 0)
        def _():
            line_copy(0, k, own.at[pl.ds(2 * part, 2), mine, :], pl.ds(2 * (part % 2), 2), (part // 2) * 4 + z).start()

        for h in range(2):
            block = 2 * part + h
            l = (block % 4 + 4 - z) % 4

            @pl.when(l != 0)
            def _(block=block, l=l):
                line_copy(1, l, own.at[pl.ds(block, 1), mine, :], pl.ds(block // 4, 1), x * 4 + block % 4).start()

    def spread_all(p, slot):
        to = line[p](slot + 1)
        return line_copy(p, slot + 1, sfar.at[p, slot, :, mine, :], slice(None), to)

    def project(i):
        for load in weight_loads(i):
            load.wait()
        slot, part = i % WSLOTS, slices[i]

        def step(n, carry):
            left = jnp.concatenate([own[2 * part], own[2 * part + 1]], axis=1)
            p, m = n // (1024 // 1024), n % (1024 // 1024)
            cols = pl.ds(pl.multiple_of(m * 1024, 1024), 1024)
            value = jnp.dot(left, weights[slot, p, :, cols], preferred_element_type=F32)
            for b in range(1024 // 256):
                j = m * (1024 // 256) + b
                v = value[:, 256 * b:256 * b + 256]
                if i > 0:
                    v = acc[p, j, :rows, :] + v
                acc[p, j, :rows, :] = v
            return carry

        lax.fori_loop(0, 2, step, 0)
        if i + WSLOTS < len(slices):
            for load in weight_loads(i + WSLOTS):
                load.start()

    spread(tp)
    project(0)
    for q in range(4):
        gather[q][2].arrived()
    spread(partner)
    project(1)
    for q in range(4):
        gather[q][0].arrived()
        if q < 2:
            pass_on(q, 3, at_y(-1), at_y(1))
        pass_on(q, 4, at_y(-1), partner)
        gather[q][1].arrived()
        if q >= 2:
            pass_on(q, 3, at_y(1), at_y(-1))
        pass_on(q, 5, at_y(1), partner)
    spread(at_y(-1))
    spread(at_y(1))
    project(2)
    project(3)
    for q in range(4):
        gather[q][4].arrived()
        gather[q][5].arrived()
    spread(at_y(-1, other))
    spread(at_y(1, other))
    project(4)
    for q in range(4):
        gather[q][3].arrived()
        pass_on(q, 6, at_y(2), partner)
    spread(at_y(2))
    project(5)
    for q in range(4):
        gather[q][6].arrived()
    spread(at_y(2, other))
    for load in loads[1:]:
        load.wait()
    for i in (6, 7):
        for load in weight_loads(i):
            load.wait()

    second = {}

    def part_of(p, origin, js=None):
        span = pl.ds(pl.multiple_of(origin * 64, 64), 64)
        return sfar.at[p, :, :, span, :] if js is None else sfar.at[p, :, js, span, :]

    def hand(p, i, origin, to, js=None):
        piece = part_of(p, origin, js)
        second[p, i] = Send(piece, piece, (d_send, d_recv), (p, i), me, to).start()

    def second_own(p):
        for slot in range(3):
            spread_all(p, slot).wait_recv()
        for i, t in enumerate((at_y(1), at_y(-1), partner)):
            hand(p, i, tp, t)

    def second_near(p):
        second[p, 0].arrived()
        hand(p, 3, at_y(-1), at_y(1), pl.ds(0, 2))
        hand(p, 4, at_y(-1), partner)
        second[p, 1].arrived()
        hand(p, 7, at_y(1), at_y(-1), pl.ds(2, 2))
        hand(p, 5, at_y(1), partner)

    def second_far(p):
        second[p, 3].arrived()
        second[p, 7].arrived()
        hand(p, 6, at_y(2), partner)

    def second_all(p):
        for i in (2, 4, 5, 6):
            second[p, i].arrived()

    length, offset = len_ref[me], off_ref[me]
    shared = {}
    view = own.reshape(4, 4, rows, 256)
    for chunk in range(4):
        last = jnp.concatenate([view[ring(y, 2), b] for b in range(4)], axis=1)
        for p in range(2):
            part = weights[6 - WSLOTS:8 - WSLOTS, p, :, 256 * chunk:256 * chunk + 256].reshape(4 * 256, 256)
            value = acc[p, chunk, :rows, :] + jnp.dot(last, part, preferred_element_type=F32)
            kv[p, :, 256 * chunk:256 * chunk + 256] = value.astype(BF16)

        for piece in (2 * chunk, 2 * chunk + 1):
            cols = pl.ds(HEAD_DIM * piece, HEAD_DIM)
            qg, kg, vg = attention_head(queries[:, cols], kv[0, :, cols], kv[1, :, cols], grads[:, cols], length, offset)
            qg_out[:, cols] = qg
            gown[0, cols, :] = kg
            gown[1, cols, :] = vg
            for p in range(2):
                for side, (k, slot) in enumerate(((1, 0), (-1, 2))):
                    shared[p, piece, side] = Send(gown.at[p, cols, :], gfar.at[p, slot, cols, :], (g_send, g_recv),
                                                  (p, piece, side), line[p](k), tp).start()
        if chunk == 0:
            second_own(0)
            second_own(1)


    passed = {}

    def forward(*pieces):
        for piece in pieces:
            side = 0 if piece < 4 else 1
            k, slot = ((1, 0), (-1, 2))[side]
            span = pl.ds(HEAD_DIM * piece, HEAD_DIM)
            for p in range(2):
                shared[p, piece, side].arrived()
                passed[p, piece] = Send(gfar.at[p, slot, span, :], gfar.at[p, 1, span, :], (f_send, f_recv), (p, piece),
                                        line[p](k), tp).start()

    def multiply(p, grad, state, first=False):
        def step(j, carry):
            value = jnp.dot(grad[...], state(j), preferred_element_type=F32)
            acc[p, j] = value if first else acc[p, j] + value
            return carry

        lax.fori_loop(0, 4, step, 0)

    def mine_for(p):
        return (lambda j: own[4 * x + j]) if p == 0 else (lambda j: own[4 * j + z])

    def theirs(p, slot):
        return lambda j: sfar[p, slot, j]

    def near_grads(p):
        for side in range(2):
            for piece in range(8):
                if (piece < 4) != (side == 0):
                    shared[p, piece, side].arrived()

    def near_block(p, k):
        j = ring(cross_spot[p], k)

        def step(half, carry):
            span = pl.ds(pl.multiple_of(half * 512, 512), 512)
            value = jnp.dot(gfar[p, 0, span, :], sfar[p, 0, j], preferred_element_type=F32)
            value = value + jnp.dot(gfar[p, 2, span, :], sfar[p, 2, j], preferred_element_type=F32)
            acc[p, j, span, :] = acc[p, j, span, :] + value
            return carry

        lax.fori_loop(0, 2, step, 0)

    multiply(0, gown.at[0], mine_for(0), True)
    second_near(0)
    multiply(1, gown.at[1], mine_for(1), True)
    forward(0, 1, 2, 3, 4, 5)
    second_near(1)
    forward(6, 7)
    second_far(0)
    second_all(0)
    near_grads(0)
    for k in (2, 1, -1):
        near_block(0, k)
    second_far(1)
    second_all(1)
    near_grads(1)
    near_block(1, 2)


    def total(p, k, c):
        j, span = ring(cross_spot[p], k), pl.ds(256 * c, 256)
        return acc[p, j, span, :] + jnp.dot(gfar[p, 1, span, :], sfar[p, 1, j], preferred_element_type=F32)

    sums = {}
    toward = (1, 1, -1, -1)

    def give_near(p, k, c):
        side = 0 if k == 1 else 1
        sums[p, side, c] = Send(near_out.at[p, side, c], near_in.at[p, side, c], (n_send, n_recv), (p, 4 * side + c),
                                cross[p](k), tp).start()

    orders = ((0, 2), (1, 3))
    for order in orders:
        for p in range(2):
            for c in order:
                passed[p, 2 * c].arrived()
                passed[p, 2 * c + 1].arrived()
                far_out[p, c] = total(p, 2, c).astype(BF16)
                sums[p, c] = Send(far_out.at[p, c], far_in.at[p, c], (r_send, r_recv), (p, c), cross[p](toward[c]), tp).start()
        for p in range(2):
            if order == orders[0] and p == 1:
                near_block(1, 1)
                near_block(1, -1)
            for c in order:
                near_out[p, (1 + toward[c]) // 2, c] = total(p, -toward[c], c).astype(BF16)
                give_near(p, -toward[c], c)
    for order in orders:
        for p in range(2):
            for c in order:
                acc[p, ring(cross_spot[p], toward[c]), pl.ds(256 * c, 256), :] = total(p, toward[c], c)
    for order in orders:
        for p in range(2):
            for c in order:
                k = toward[c]
                sums[p, c].arrived()
                value = acc[p, ring(cross_spot[p], k), pl.ds(256 * c, 256), :] + far_in[p, c].astype(F32)
                near_out[p, (1 - k) // 2, c] = value.astype(BF16)
                give_near(p, k, c)
    for p in range(2):
        near_block(p, 0)
        for c in range(4):
            acc[p, cross_spot[p], pl.ds(256 * c, 256), :] = total(p, 0, c)
    for order in orders:
        for p, out in enumerate((kw_out, vw_out)):
            for c in order:
                sums[p, 0, c].arrived()
                sums[p, 1, c].arrived()
                value = acc[p, cross_spot[p], pl.ds(256 * c, 256), :] + near_in[p, 0, c].astype(F32)
                value = value + near_in[p, 1, c].astype(F32)
                out[:, 256 * c:256 * c + 256] = value.T.astype(BF16)

    for p in range(2):
        for slot in range(3):
            spread_all(p, slot).wait_send()
    drain()


def hand_over(*refs):
    copies = [pltpu.make_async_copy(refs[i], refs[3 + i], refs[6].at[i]) for i in range(3)]
    for copy in copies:
        copy.start()
    for copy in copies:
        copy.wait()


def shards(queries, states, state_doc, state_pos, lengths, offsets, key_weight, value_weight, context_grad):
    docs = lax.axis_size("seq")
    parts = lax.axis_size("tp")
    rows, features = states.shape
    count, width = queries.shape
    any_spec = pl.BlockSpec(memory_space=pl.ANY)
    vmem_spec = pl.BlockSpec(memory_space=pltpu.VMEM)
    smem_spec = pl.BlockSpec(memory_space=pltpu.SMEM)
    dma = pltpu.SemaphoreType.DMA
    pair = lambda *shape: [dma(shape), dma(shape)]
    results = pl.pallas_call(
        functools.partial(kernel, docs),
        out_shape=[pltpu.VMEM((count, width), BF16)] + [pltpu.VMEM((256, width), BF16)] * 2,
        in_specs=[vmem_spec, vmem_spec, smem_spec, smem_spec] + [any_spec] * 5,
        out_specs=[vmem_spec] * 3,
        scratch_shapes=[
            pltpu.VMEM((rows, features), BF16),
            pltpu.VMEM((count, width), BF16),
            pltpu.VMEM((count, width), BF16),
            pltpu.VMEM((WSLOTS, 2, features, width), BF16),
            pltpu.VMEM((4, docs, SLOTS, 128), BF16),
            pltpu.VMEM((4, docs, SLOTS, 128), BF16),
            pltpu.VMEM((16, rows, 256), BF16),
            pltpu.VMEM((2, 4, width, 256), F32),
            pltpu.VMEM((2, rows, width), BF16),
            pltpu.VMEM((2, width, rows), BF16),
            pltpu.VMEM((2, 3, width, rows), BF16),
            pltpu.VMEM((2, 3, 4, rows, 256), BF16),
            pltpu.VMEM((2, 4, 256, 256), BF16),
            pltpu.VMEM((2, 4, 256, 256), BF16),
            pltpu.VMEM((2, 2, 4, 256, 256), BF16),
            pltpu.VMEM((2, 2, 4, 256, 256), BF16),
            dma((3,)), dma((WSLOTS, 2)),
            *pair(4, docs), *pair(4, 7), *pair(2, 3), *pair(2, 8),
            *pair(2, 8, 2), *pair(2, 8), *pair(2, 4), *pair(2, 8),
        ],
        compiler_params=pltpu.CompilerParams(collective_id=0, has_side_effects=True, vmem_limit_bytes=60 << 20),
        name="routed",
    )(state_doc.reshape(-1, 128), state_pos.reshape(-1, 128), lengths, offsets, queries, states,
      key_weight.reshape(parts, features, width), value_weight.reshape(parts, features, width), context_grad)
    return pl.pallas_call(
        hand_over,
        out_shape=[jax.ShapeDtypeStruct((256, width), BF16)] * 3,
        in_specs=[vmem_spec] * 3,
        out_specs=[any_spec] * 3,
        scratch_shapes=[dma((3,))],
        compiler_params=pltpu.CompilerParams(vmem_limit_bytes=4 << 20),
        name="hand_over",
    )(*results)


def solution(mesh):
    in_specs = (P("seq", "tp"), P("seq", "tp"), P(), P(), P(), P(), P(None, "tp"), P(None, "tp"), P("seq", "tp"))
    out_specs = (P("seq", "tp"), P("seq", "tp"), P("seq", "tp"))
    return jax.shard_map(shards, mesh=mesh, in_specs=in_specs, out_specs=out_specs, check_vma=False)
```

```python
import functools

import jax
import jax.numpy as jnp
from jax import lax
from jax.experimental import pallas as pl
from jax.experimental.pallas import tpu as pltpu
from jax.sharding import PartitionSpec as P

HEAD_DIM = 128
SLOTS = 64
USED = 56
F32 = jnp.float32
BF16 = jnp.bfloat16


def dot_nt(a, b):
    return lax.dot_general(a, b, (((1,), (1,)), ((), ())), preferred_element_type=F32)


def dot_tn(a, b):
    return lax.dot_general(a, b, (((0,), (0,)), ((), ())), preferred_element_type=F32)


def strict_upper(n):
    return (lax.broadcasted_iota(jnp.int32, (n, n), 0) < lax.broadcasted_iota(jnp.int32, (n, n), 1)).astype(F32).astype(BF16)


def pack_table(doc_ref, me, docs, rows):
    own = jnp.concatenate([doc_ref[pl.ds(4 * me + j, 1), :] for j in range(4)], axis=1)
    member = lax.broadcasted_iota(jnp.int32, (docs, rows), 0) == own
    member_f = member.astype(F32)
    ranks = jnp.dot(member_f.astype(BF16), strict_upper(rows), preferred_element_type=F32)
    rank = jnp.sum(ranks * member_f, axis=0, keepdims=True).astype(jnp.int32)
    target = own * SLOTS + rank
    hot = lax.broadcasted_iota(jnp.int32, (docs * SLOTS, rows), 0) == target
    return hot.astype(F32).astype(BF16)


def order_table(doc_ref, pos_ref, me, docs, rows):
    docs_all = jnp.concatenate([doc_ref[pl.ds(j, docs, stride=4), :] for j in range(4)], axis=1)
    pos_all = jnp.concatenate([pos_ref[pl.ds(j, docs, stride=4), :] for j in range(4)], axis=1)
    member = docs_all == me
    member_f = member.astype(F32)
    ranks = jnp.dot(member_f.astype(BF16), strict_upper(rows), preferred_element_type=F32).astype(jnp.int32)
    ranks = jnp.where(member, ranks, -1)
    high = (pos_all // 2).astype(F32)
    low = (pos_all % 2).astype(F32)
    parts = []
    for s in range(docs):
        hot = (lax.broadcasted_iota(jnp.int32, (SLOTS, rows), 0) == ranks[s:s + 1, :]).astype(F32).astype(BF16)
        three = jnp.concatenate([high[s:s + 1], low[s:s + 1], jnp.ones((1, rows), F32), jnp.zeros((5, rows), F32)], axis=0)
        parts.append(dot_nt(three.astype(BF16), hot))
    table = jnp.concatenate(parts, axis=1)
    slot_pos = (2.0 * table[0:1] + table[1:2] + table[2:3]).astype(jnp.int32) - 1
    hot = lax.broadcasted_iota(jnp.int32, (rows, docs * SLOTS), 0) == slot_pos
    return hot.astype(F32).astype(BF16)


def attention_head(q, k, v, g, length, offset):
    scale = HEAD_DIM ** (-0.5)
    queries, rows = q.shape[0], k.shape[0]
    scores = dot_nt(q, k) * scale
    index = lax.broadcasted_iota(jnp.int32, (queries, rows), 0)
    pos = lax.broadcasted_iota(jnp.int32, (queries, rows), 1)
    visible = (pos <= index + offset) & (pos < length)
    scores = jnp.where(visible, scores, -jnp.inf)
    weights = jnp.exp(scores - jnp.max(scores, axis=1, keepdims=True))
    probs = weights * (1.0 / jnp.sum(weights, axis=1, keepdims=True))
    low = probs.astype(BF16)
    prob_grad = dot_nt(g, v)
    delta = jnp.sum(low.astype(F32) * prob_grad, axis=1, keepdims=True)
    score_grad = (probs * (prob_grad - delta) * scale).astype(BF16)
    q_grad = jnp.dot(score_grad, k, preferred_element_type=F32).astype(BF16)
    k_grad = dot_tn(q, score_grad).astype(BF16)
    v_grad = dot_tn(g, low).astype(BF16)
    return q_grad, k_grad, v_grad


MESH = pl.DeviceIdType.MESH
WSLOTS = 5
STARTED = []


class Send:
    def __init__(self, src, dst, sems, index, seq, tp):
        send, recv = sems
        self.copy = pltpu.make_async_remote_copy(
            src_ref=src, dst_ref=dst, send_sem=send.at[index], recv_sem=recv.at[index],
            device_id={"seq": seq, "tp": tp}, device_id_type=MESH)
        self.waited = False

    def start(self):
        self.copy.start()
        STARTED.append(self)
        return self

    def arrived(self):
        self.copy.wait_recv()
        self.waited = True

    def finish(self):
        if not self.waited:
            self.arrived()
        self.copy.wait_send()


def kernel(docs, doc_ref, pos_ref, len_ref, off_ref, q_hbm, s_hbm, wk_hbm, wv_hbm, g_hbm,
           qg_out, kw_out, vw_out,
           states, queries, grads, weights, packed, arrived, own, acc, kv, gown, gfar, sfar,
           far_out, far_in, near_out, near_in,
           load_sem, w_sem, a_send, a_recv, b_send, b_recv, c_send, c_recv, d_send, d_recv,
           g_send, g_recv, f_send, f_recv, r_send, r_recv, n_send, n_recv):
    STARTED.clear()

    def drain():
        for send in STARTED:
            send.finish()

    rows = states.shape[0]
    me, tp = lax.axis_index("seq"), lax.axis_index("tp")
    x, z = me // 4, me % 4
    y, core = tp // 2, tp % 2

    def ring(v, k):
        return (v + k % 4) % 4

    def at_x(k):
        return ring(x, k) * 4 + z

    def at_z(k):
        return x * 4 + ring(z, k)

    def at_y(k, c=None):
        return ring(y, k) * 2 + (core if c is None else c)

    other = 1 - core
    partner = y * 2 + other
    line = (at_x, at_z)
    cross = (at_z, at_x)
    spot = (x, z)
    cross_spot = (z, x)

    loads = [pltpu.make_async_copy(s, d, load_sem.at[i])
             for i, (s, d) in enumerate(((s_hbm, states), (q_hbm, queries), (g_hbm, grads)))]
    for load in loads:
        load.start()
    slices = [at_y(0), partner, at_y(-1), at_y(1), at_y(-1, other), at_y(1, other), at_y(2, 0), at_y(2, 1)]

    def weight_loads(i):
        slot = i % WSLOTS
        return [pltpu.make_async_copy(w.at[slices[i]], weights.at[slot, p], w_sem.at[slot, p])
                for p, w in enumerate((wk_hbm, wv_hbm))]

    for i in range(WSLOTS):
        for load in weight_loads(i):
            load.start()

    arrived[:, :, 48:, :] = jnp.zeros((4, docs, SLOTS - 48, 128), BF16)

    barrier = pltpu.get_barrier_semaphore()
    for k in range(1, docs):
        pl.semaphore_signal(barrier, inc=1, device_id={"seq": (me + k) % docs, "tp": tp}, device_id_type=MESH)
    for t in (at_y(1), at_y(-1), partner):
        pl.semaphore_signal(barrier, inc=1, device_id={"seq": me, "tp": t}, device_id_type=MESH)

    table = pack_table(doc_ref, me, docs, rows)
    loads[0].wait()
    for h in range(2):
        block = jnp.dot(table, states[:, 256 * h:256 * h + 256], preferred_element_type=F32).astype(BF16)
        packed[2 * h] = block[:, :128].reshape(docs, SLOTS, 128)
        packed[2 * h + 1] = block[:, 128:].reshape(docs, SLOTS, 128)
    pl.semaphore_wait(barrier, docs - 1 + 3)
    peers = sorted(((i, j) for i in range(4) for j in range(4) if i or j), key=lambda d: min(d[0], 4 - d[0]) + min(d[1], 4 - d[1]))
    routes = [[], [], [], []]
    for q in range(4):
        for k, (i, j) in enumerate(peers):
            to = ring(x, i) * 4 + ring(z, j)
            routes[q].append(Send(packed.at[q, to, pl.ds(0, USED)], arrived.at[q, me, pl.ds(0, USED)], (a_send, a_recv),
                                  (q, k), to, tp).start())
        arrived[q, me] = packed[q, me]
    table = order_table(doc_ref, pos_ref, me, docs, rows)

    gather = [{}, {}, {}, {}]

    def pass_on(q, i, origin, to):
        piece = own.at[2 * origin + q // 2, :, pl.ds(128 * (q % 2), 128)]
        gather[q][i] = Send(piece, piece, (b_send, b_recv), (q, i), me, to).start()

    for q in range(4):
        for route in routes[q]:
            route.arrived()
        value = jnp.dot(table, arrived[q].reshape(docs * SLOTS, 128), preferred_element_type=F32)
        own[2 * tp + q // 2, :, 128 * (q % 2):128 * (q % 2) + 128] = value.astype(BF16)
        for i, t in enumerate((at_y(1), at_y(-1), partner)):
            pass_on(q, i, tp, t)

    mine = pl.ds(pl.multiple_of(tp * 64, 64), 64)

    def line_copy(p, k, src, js, to):
        return pltpu.make_async_remote_copy(
            src_ref=src, dst_ref=sfar.at[p, k - 1, js, mine, :], send_sem=c_send.at[p, k - 1], recv_sem=c_recv.at[p, k - 1],
            device_id={"seq": to, "tp": tp}, device_id_type=MESH)

    def spread(part):
        k = (part // 2 + 4 - x) % 4

        @pl.when(k != 0)
        def _():
            line_copy(0, k, own.at[pl.ds(2 * part, 2), mine, :], pl.ds(2 * (part % 2), 2), (part // 2) * 4 + z).start()

        for h in range(2):
            block = 2 * part + h
            l = (block % 4 + 4 - z) % 4

            @pl.when(l != 0)
            def _(block=block, l=l):
                line_copy(1, l, own.at[pl.ds(block, 1), mine, :], pl.ds(block // 4, 1), x * 4 + block % 4).start()

    def spread_all(p, slot):
        to = line[p](slot + 1)
        return line_copy(p, slot + 1, sfar.at[p, slot, :, mine, :], slice(None), to)

    def project(i):
        for load in weight_loads(i):
            load.wait()
        slot, part = i % WSLOTS, slices[i]

        def step(n, carry):
            left = jnp.concatenate([own[2 * part], own[2 * part + 1]], axis=1)
            p, m = n // (1024 // 1024), n % (1024 // 1024)
            cols = pl.ds(pl.multiple_of(m * 1024, 1024), 1024)
            value = jnp.dot(left, weights[slot, p, :, cols], preferred_element_type=F32)
            for b in range(1024 // 256):
                j = m * (1024 // 256) + b
                v = value[:, 256 * b:256 * b + 256]
                if i > 0:
                    v = acc[p, j, :rows, :] + v
                acc[p, j, :rows, :] = v
            return carry

        lax.fori_loop(0, 2, step, 0)
        if i + WSLOTS < len(slices):
            for load in weight_loads(i + WSLOTS):
                load.start()

    spread(tp)
    project(0)
    for q in range(4):
        gather[q][2].arrived()
    spread(partner)
    project(1)
    for q in range(4):
        gather[q][0].arrived()
        if q < 2:
            pass_on(q, 3, at_y(-1), at_y(1))
        pass_on(q, 4, at_y(-1), partner)
        gather[q][1].arrived()
        if q >= 2:
            pass_on(q, 3, at_y(1), at_y(-1))
        pass_on(q, 5, at_y(1), partner)
    spread(at_y(-1))
    spread(at_y(1))
    project(2)
    project(3)
    for q in range(4):
        gather[q][4].arrived()
        gather[q][5].arrived()
    spread(at_y(-1, other))
    spread(at_y(1, other))
    project(4)
    for q in range(4):
        gather[q][3].arrived()
        pass_on(q, 6, at_y(2), partner)
    spread(at_y(2))
    project(5)
    for q in range(4):
        gather[q][6].arrived()
    spread(at_y(2, other))
    for load in loads[1:]:
        load.wait()
    for i in (6, 7):
        for load in weight_loads(i):
            load.wait()

    second = {}

    def part_of(p, origin, js=None):
        span = pl.ds(pl.multiple_of(origin * 64, 64), 64)
        return sfar.at[p, :, :, span, :] if js is None else sfar.at[p, :, js, span, :]

    def hand(p, i, origin, to, js=None):
        piece = part_of(p, origin, js)
        second[p, i] = Send(piece, piece, (d_send, d_recv), (p, i), me, to).start()

    def second_own(p):
        for slot in range(3):
            spread_all(p, slot).wait_recv()
        for i, t in enumerate((at_y(1), at_y(-1), partner)):
            hand(p, i, tp, t)

    def second_near(p):
        second[p, 0].arrived()
        hand(p, 3, at_y(-1), at_y(1), pl.ds(0, 2))
        hand(p, 4, at_y(-1), partner)
        second[p, 1].arrived()
        hand(p, 7, at_y(1), at_y(-1), pl.ds(2, 2))
        hand(p, 5, at_y(1), partner)

    def second_far(p):
        second[p, 3].arrived()
        second[p, 7].arrived()
        hand(p, 6, at_y(2), partner)

    def second_all(p):
        for i in (2, 4, 5, 6):
            second[p, i].arrived()

    length, offset = len_ref[me], off_ref[me]
    shared = {}
    view = own.reshape(4, 4, rows, 256)
    for chunk in range(4):
        last = jnp.concatenate([view[ring(y, 2), b] for b in range(4)], axis=1)
        for p in range(2):
            part = weights[6 - WSLOTS:8 - WSLOTS, p, :, 256 * chunk:256 * chunk + 256].reshape(4 * 256, 256)
            value = acc[p, chunk, :rows, :] + jnp.dot(last, part, preferred_element_type=F32)
            kv[p, :, 256 * chunk:256 * chunk + 256] = value.astype(BF16)

        for piece in (2 * chunk, 2 * chunk + 1):
            cols = pl.ds(HEAD_DIM * piece, HEAD_DIM)
            qg, kg, vg = attention_head(queries[:, cols], kv[0, :, cols], kv[1, :, cols], grads[:, cols], length, offset)
            qg_out[:, cols] = qg
            gown[0, cols, :] = kg
            gown[1, cols, :] = vg
            for p in range(2):
                for side, (k, slot) in enumerate(((1, 0), (-1, 2))):
                    shared[p, piece, side] = Send(gown.at[p, cols, :], gfar.at[p, slot, cols, :], (g_send, g_recv),
                                                  (p, piece, side), line[p](k), tp).start()
        if chunk == 0:
            second_own(0)
            second_own(1)


    passed = {}

    def forward(*pieces):
        for piece in pieces:
            side = 0 if piece < 4 else 1
            k, slot = ((1, 0), (-1, 2))[side]
            span = pl.ds(HEAD_DIM * piece, HEAD_DIM)
            for p in range(2):
                shared[p, piece, side].arrived()
                passed[p, piece] = Send(gfar.at[p, slot, span, :], gfar.at[p, 1, span, :], (f_send, f_recv), (p, piece),
                                        line[p](k), tp).start()

    def multiply(p, grad, state, first=False):
        def step(j, carry):
            value = jnp.dot(grad[...], state(j), preferred_element_type=F32)
            acc[p, j] = value if first else acc[p, j] + value
            return carry

        lax.fori_loop(0, 4, step, 0)

    def mine_for(p):
        return (lambda j: own[4 * x + j]) if p == 0 else (lambda j: own[4 * j + z])

    def theirs(p, slot):
        return lambda j: sfar[p, slot, j]

    def near_grads(p):
        for side in range(2):
            for piece in range(8):
                if (piece < 4) != (side == 0):
                    shared[p, piece, side].arrived()

    def near_block(p, k):
        j = ring(cross_spot[p], k)

        def step(half, carry):
            span = pl.ds(pl.multiple_of(half * 512, 512), 512)
            value = jnp.dot(gfar[p, 0, span, :], sfar[p, 0, j], preferred_element_type=F32)
            value = value + jnp.dot(gfar[p, 2, span, :], sfar[p, 2, j], preferred_element_type=F32)
            acc[p, j, span, :] = acc[p, j, span, :] + value
            return carry

        lax.fori_loop(0, 2, step, 0)

    multiply(0, gown.at[0], mine_for(0), True)
    second_near(0)
    multiply(1, gown.at[1], mine_for(1), True)
    forward(0, 1, 2, 3, 4, 5)
    second_near(1)
    forward(6, 7)
    second_far(0)
    second_all(0)
    near_grads(0)
    near_block(0, 2)
    second_far(1)
    near_block(0, 1)
    near_block(0, -1)
    second_all(1)
    near_grads(1)
    near_block(1, 2)


    def total(p, k, c):
        j, span = ring(cross_spot[p], k), pl.ds(256 * c, 256)
        return acc[p, j, span, :] + jnp.dot(gfar[p, 1, span, :], sfar[p, 1, j], preferred_element_type=F32)

    sums = {}
    toward = (1, 1, -1, -1)

    def give_near(p, k, c):
        side = 0 if k == 1 else 1
        sums[p, side, c] = Send(near_out.at[p, side, c], near_in.at[p, side, c], (n_send, n_recv), (p, 4 * side + c),
                                cross[p](k), tp).start()

    orders = ((0, 2), (1, 3))
    for order in orders:
        for p in range(2):
            for c in order:
                passed[p, 2 * c].arrived()
                passed[p, 2 * c + 1].arrived()
                far_out[p, c] = total(p, 2, c).astype(BF16)
                sums[p, c] = Send(far_out.at[p, c], far_in.at[p, c], (r_send, r_recv), (p, c), cross[p](toward[c]), tp).start()
        for p in range(2):
            if order == orders[0] and p == 1:
                near_block(1, 1)
                near_block(1, -1)
            for c in order:
                near_out[p, (1 + toward[c]) // 2, c] = total(p, -toward[c], c).astype(BF16)
                give_near(p, -toward[c], c)
    for order in orders:
        for p in range(2):
            for c in order:
                acc[p, ring(cross_spot[p], toward[c]), pl.ds(256 * c, 256), :] = total(p, toward[c], c)
    for order in orders:
        for p in range(2):
            for c in order:
                k = toward[c]
                sums[p, c].arrived()
                value = acc[p, ring(cross_spot[p], k), pl.ds(256 * c, 256), :] + far_in[p, c].astype(F32)
                near_out[p, (1 - k) // 2, c] = value.astype(BF16)
                give_near(p, k, c)
    for p in range(2):
        near_block(p, 0)
        for c in range(4):
            acc[p, cross_spot[p], pl.ds(256 * c, 256), :] = total(p, 0, c)
    for order in orders:
        for p, out in enumerate((kw_out, vw_out)):
            for c in order:
                sums[p, 0, c].arrived()
                sums[p, 1, c].arrived()
                value = acc[p, cross_spot[p], pl.ds(256 * c, 256), :] + near_in[p, 0, c].astype(F32)
                value = value + near_in[p, 1, c].astype(F32)
                out[:, 256 * c:256 * c + 256] = value.T.astype(BF16)

    for p in range(2):
        for slot in range(3):
            spread_all(p, slot).wait_send()
    drain()


def hand_over(*refs):
    copies = [pltpu.make_async_copy(refs[i], refs[3 + i], refs[6].at[i]) for i in range(3)]
    for copy in copies:
        copy.start()
    for copy in copies:
        copy.wait()


def shards(queries, states, state_doc, state_pos, lengths, offsets, key_weight, value_weight, context_grad):
    docs = lax.axis_size("seq")
    parts = lax.axis_size("tp")
    rows, features = states.shape
    count, width = queries.shape
    any_spec = pl.BlockSpec(memory_space=pl.ANY)
    vmem_spec = pl.BlockSpec(memory_space=pltpu.VMEM)
    smem_spec = pl.BlockSpec(memory_space=pltpu.SMEM)
    dma = pltpu.SemaphoreType.DMA
    pair = lambda *shape: [dma(shape), dma(shape)]
    results = pl.pallas_call(
        functools.partial(kernel, docs),
        out_shape=[pltpu.VMEM((count, width), BF16)] + [pltpu.VMEM((256, width), BF16)] * 2,
        in_specs=[vmem_spec, vmem_spec, smem_spec, smem_spec] + [any_spec] * 5,
        out_specs=[vmem_spec] * 3,
        scratch_shapes=[
            pltpu.VMEM((rows, features), BF16),
            pltpu.VMEM((count, width), BF16),
            pltpu.VMEM((count, width), BF16),
            pltpu.VMEM((WSLOTS, 2, features, width), BF16),
            pltpu.VMEM((4, docs, SLOTS, 128), BF16),
            pltpu.VMEM((4, docs, SLOTS, 128), BF16),
            pltpu.VMEM((16, rows, 256), BF16),
            pltpu.VMEM((2, 4, width, 256), F32),
            pltpu.VMEM((2, rows, width), BF16),
            pltpu.VMEM((2, width, rows), BF16),
            pltpu.VMEM((2, 3, width, rows), BF16),
            pltpu.VMEM((2, 3, 4, rows, 256), BF16),
            pltpu.VMEM((2, 4, 256, 256), BF16),
            pltpu.VMEM((2, 4, 256, 256), BF16),
            pltpu.VMEM((2, 2, 4, 256, 256), BF16),
            pltpu.VMEM((2, 2, 4, 256, 256), BF16),
            dma((3,)), dma((WSLOTS, 2)),
            *pair(4, docs), *pair(4, 7), *pair(2, 3), *pair(2, 8),
            *pair(2, 8, 2), *pair(2, 8), *pair(2, 4), *pair(2, 8),
        ],
        compiler_params=pltpu.CompilerParams(collective_id=0, has_side_effects=True, vmem_limit_bytes=60 << 20),
        name="routed",
    )(state_doc.reshape(-1, 128), state_pos.reshape(-1, 128), lengths, offsets, queries, states,
      key_weight.reshape(parts, features, width), value_weight.reshape(parts, features, width), context_grad)
    return pl.pallas_call(
        hand_over,
        out_shape=[jax.ShapeDtypeStruct((256, width), BF16)] * 3,
        in_specs=[vmem_spec] * 3,
        out_specs=[any_spec] * 3,
        scratch_shapes=[dma((3,))],
        compiler_params=pltpu.CompilerParams(vmem_limit_bytes=4 << 20),
        name="hand_over",
    )(*results)


def solution(mesh):
    in_specs = (P("seq", "tp"), P("seq", "tp"), P(), P(), P(), P(), P(None, "tp"), P(None, "tp"), P("seq", "tp"))
    out_specs = (P("seq", "tp"), P("seq", "tp"), P("seq", "tp"))
    return jax.shard_map(shards, mesh=mesh, in_specs=in_specs, out_specs=out_specs, check_vma=False)
```
